512 devices in a mesh: section: 4 (over x), dp: 4 (over y), tensor: 32 (over z, core).
Axes of the slice: x: 4, y: 4, z: 16, core: 2. Of those that a mesh axis runs over, the one named last changes fastest.
Arguments:
- activations: bfloat16 [512, 8192], P('dp', 'tensor'), may hold values from -6 to 6
- targets: bfloat16 [4, 512, 8192], P('section', 'dp', 'tensor'), may hold values from -12 to 12
- packed_floors: int32 [4, 2048, 8192], P('section', 'dp', 'tensor'), may hold values from 0 to 4095
- rounding: float32 [4, 8192, 8192], P('section', 'dp', 'tensor'), may hold values from -8 to 8
- scales: float32 [4, 8192], P('section', 'tensor'), may hold values from 0.001 to 0.006
- norm_gains: float32 [4, 8192], P('section'), may hold values from 0.5 to 1.5
Outputs:
- rounding_next: float32 [4, 8192, 8192], P('section', 'dp', 'tensor')
- block_outputs: bfloat16 [4, 512, 8192], P('section', 'dp', 'tensor')
- losses: float32 [4], P('section')
The draws below stay inside these ranges and needn't reach their ends.
Inputs may be any that keep to these rules, and one draw needn't show every extreme that they name: `packed_floors`: each word holds four 3-bit codes in its lowest 12 bits, lowest bits first: code k of word r of a column is row 4 r + k; the floor is the code minus 4.
All inputs are finite; a program needn't handle non-finite values.
Results may differ from the reference program's by a relative error of at most 0.0045.
The reference program's roundings to bfloat16 on the way count: a program that leaves them out, or rounds other values in their place, can miss the bound.
Values may be sent and summed in bfloat16 or wider, within the bound.
No kernel may reach another device: no remote copies, remote signals or barrier semaphores. Data moves between devices by JAX's collectives and lax.ppermute only.
A program may use at most 64 MiB of HBM per device.

```python
import math
import jax
import jax.numpy as jnp
from jax import lax

D = 8192
TOKENS = 512
N_SECTION = 4


def draw_rounding(key, part):
    key_base = jax.random.fold_in(key, 11)
    key_rows = jax.random.fold_in(key, 12)
    key_cols = jax.random.fold_in(key, 13)
    positions = jnp.arange(D, dtype=jnp.float32) / (D - 1)
    row_level = positions[None, :, None] * jnp.ones((N_SECTION, D, 1), jnp.float32)
    col_level = positions[None, None, :] * jnp.ones((N_SECTION, 1, D), jnp.float32)
    row_rough = jax.random.uniform(key_rows, (N_SECTION, D, 1), jnp.float32, 0.6, 1.5)
    col_rough = jax.random.uniform(key_cols, (N_SECTION, 1, D), jnp.float32, 0.6, 1.5)
    spread = 0.15 * jnp.exp(jnp.log(40.0) * 0.5 * (row_level + col_level)) * row_rough * col_rough
    base = jax.random.normal(key_base, (N_SECTION, D, D), jnp.float32)
    return jnp.clip(base * spread, -8.0, 8.0)


def plant(drawn, rng, smallest, largest):
    place = [jax.random.randint(jax.random.fold_in(rng, axis), (), 0, length) for axis, length in enumerate(drawn.shape)]
    main_axis = drawn.shape.index(max(drawn.shape))
    next_to = place[:main_axis] + [(place[main_axis] + 1) % drawn.shape[main_axis]] + place[main_axis + 1:]
    return drawn.at[tuple(place)].set(smallest).at[tuple(next_to)].set(largest)


def level_of(rng, shape, split, low, top_value):
    def one(axis_at, blocks):
        draws = jax.random.uniform(jax.random.fold_in(jax.random.fold_in(rng, 6), axis_at), (blocks,), jnp.float32, low / len(split), top_value / len(split))
        return jnp.repeat(jnp.exp(draws), shape[axis_at] // blocks).reshape((-1,) + (1,) * (len(shape) - axis_at - 1))

    loudness = one(*split[0])
    for cut in split[1:]:
        loudness = loudness * one(*cut)
    return loudness


def gaussian(own_key, dims, scale, most, pieces=(), held_as=jnp.bfloat16):
    array = scale * jax.random.normal(own_key, dims, jnp.float32)
    if pieces:
        array = array * level_of(own_key, dims, pieces, -0.22, 0.18)
    return jnp.clip(array, -most, most).astype(held_as)


def setup_inputs(seed: int = 0) -> dict:
    streams_of = jax.random.split(jax.random.key(seed), 7)
    activations = gaussian(streams_of[0], (TOKENS, D), 1.0, 6.0, ((0, 4), (1, 32)))
    targets = gaussian(streams_of[1], (N_SECTION, TOKENS, D), 2.0, 12.0, ((0, 4), (1, 4), (2, 32)))
    packed_floors = plant(jax.random.randint(streams_of[2], (N_SECTION, D // 4, D), 0, 4096), jax.random.fold_in(streams_of[2], 1), 0, 4095).astype(jnp.int32)
    rounding = draw_rounding(jax.random.fold_in(streams_of[6], 71), 0)
    scales = jnp.clip(jnp.exp(math.log(0.006) - 1.7917594 * jax.random.uniform(streams_of[4], (N_SECTION, D), jnp.float32) ** level_of(streams_of[4], (N_SECTION, D), ((0, 4), (1, 32)), -0.2, 0.2)), 0.001, 0.006)
    norm_gains = jnp.clip(1.0 + 0.1 * jax.random.normal(streams_of[5], (N_SECTION, D), jnp.float32), 0.5, 1.5)
    return {"activations": activations, "targets": targets, "packed_floors": packed_floors, "rounding": rounding, "scales": scales, "norm_gains": norm_gains}


norm_eps = 1e-06
grad_eps = 1e-06
reg_weight = 0.3
step_rate = 0.25
error_scale = 600.0

def unpack(words):
    shifts = 3 * jnp.arange(4, dtype=jnp.int32)
    codes = jnp.right_shift(words[:, None, :], shifts[None, :, None]) & 7
    return codes.reshape(words.shape[0] * 4, words.shape[1]).astype(jnp.float32) - 4.0

def soft_round(values):
    sig = jax.nn.sigmoid(values)
    linear = 1.2 * sig - 0.1
    soft_part = jnp.clip(linear, 0.0, 1.0)
    soft_slope = jnp.where((linear > 0.0) & (linear < 1.0), 1.2 * sig * (1.0 - sig), 0.0)
    return (soft_part, soft_slope)

def reference(activations, targets, packed_floors, rounding, scales, norm_gains):
    token_total, width_full = activations.shape
    current = activations
    next_list, output_list, loss_list = ([], [], [])
    for section_index in range(N_SECTION):
        floors = unpack(packed_floors[section_index])
        soft_part, soft_slope = soft_round(rounding[section_index])
        weight = (scales[section_index][None, :] * (floors + soft_part)).astype(jnp.bfloat16)
        inputs = current.astype(jnp.float32)
        mean_sq = lax.optimization_barrier(jnp.mean(inputs * inputs, axis=1, keepdims=True))
        normed = (inputs * lax.rsqrt(mean_sq + norm_eps) * norm_gains[section_index][None, :]).astype(jnp.bfloat16)
        result = (inputs + jnp.dot(normed, weight, preferred_element_type=jnp.float32)).astype(jnp.bfloat16)
        residue = result.astype(jnp.float32) - targets[section_index].astype(jnp.float32)
        delta = (error_scale / token_total ** 0.5 * residue).astype(jnp.bfloat16)
        grad_w = lax.dot_general(normed, delta, (((0,), (0,)), ((), ())), preferred_element_type=jnp.float32)
        polarity = 2.0 * soft_part - 1.0
        grad = soft_slope * (scales[section_index][None, :] * grad_w - 8.0 * reg_weight * polarity ** 3)
        mean_grad = jnp.sum(grad * grad) / (width_full * width_full) + grad_eps
        next_list.append(rounding[section_index] - step_rate * grad * lax.rsqrt(mean_grad))
        loss_list.append(jnp.sum(residue * residue) / (token_total * width_full) + reg_weight * jnp.sum(1.0 - polarity ** 4) / (width_full * width_full))
        output_list.append(result)
        current = result
    return (jnp.stack(next_list), jnp.stack(output_list), jnp.stack(loss_list))
```

```python
import jax
import jax.numpy as jnp
from jax import lax
from jax.sharding import Mesh
from jax.sharding import PartitionSpec as P

TENSOR = ("tensor_0", "tensor_1")
PLANE = ("section", "dp")

norm_eps = 1e-06
grad_eps = 1e-06
reg_weight = 0.3
step_rate = 0.25
error_scale = 600.0


def exchange(x, axes):
    return lax.all_to_all(x, axes, 0, 0, tiled=True)


def total_over(x, axes):
    peers = 1
    for axis in axes if isinstance(axes, tuple) else (axes,):
        peers *= lax.axis_size(axis)
    return jnp.sum(exchange(jnp.broadcast_to(x[None], (peers, *x.shape)), axes), axis=0)


def unpack(words):
    shifts = 3 * jnp.arange(4, dtype=jnp.int32)
    codes = jnp.right_shift(words[:, None, :], shifts[None, :, None]) & 7
    return codes.reshape(words.shape[0] * 4, words.shape[1]).astype(jnp.float32) - 4.0


def soft_round(values):
    sig = jax.nn.sigmoid(values)
    linear = 1.2 * sig - 0.1
    soft_part = jnp.clip(linear, 0.0, 1.0)
    soft_slope = jnp.where((linear > 0.0) & (linear < 1.0), 1.2 * sig * (1.0 - sig), 0.0)
    return (soft_part, soft_slope)


def per_device(activations, targets, packed_floors, rounding, scales, norm_gains):
    sections = lax.axis_size("section")
    dps = lax.axis_size("dp")
    tensors = lax.axis_size("tensor_0") * lax.axis_size("tensor_1")
    section_index = lax.axis_index("section")
    dp_index = lax.axis_index("dp")
    tok_dev, width_local = activations.shape
    width_full = norm_gains.shape[1]
    token_total = tok_dev * dps
    rows_local = width_full // dps
    near = tensors // dps
    own = width_local // dps
    tok_part = tok_dev // sections
    tok_group = tok_part * dps

    soft_part, soft_slope = soft_round(rounding[0])
    channel_scale = scales[0][None, :]
    weight = (channel_scale * (unpack(packed_floors[0]) + soft_part)).astype(jnp.bfloat16)
    weight = weight.reshape(near, dps, own, width_local).transpose(1, 0, 2, 3)
    weight = exchange(weight.reshape(dps, near * own, width_local), "dp")
    weights = lax.all_gather(weight.reshape(rows_local, width_local), "section", axis=0)

    gains_own = norm_gains[0].reshape(tensors, dps, own)
    gains_own = lax.dynamic_index_in_dim(gains_own, dp_index, 1, keepdims=False).reshape(1, rows_local)
    gains = lax.all_gather(gains_own, "section", axis=0, tiled=True)

    fresh = lax.dynamic_slice_in_dim(activations, section_index * tok_part, tok_part, 0)
    fresh = exchange(fresh.reshape(tok_part, dps, own).transpose(1, 0, 2), "dp")
    current = fresh.reshape(tok_group, own).T

    target_all = lax.all_gather(targets[0], "dp", axis=0)
    target_all = target_all.reshape(dps, sections, tok_part, width_local).transpose(1, 0, 2, 3)
    target_all = target_all.reshape(token_total, width_local).astype(jnp.float32)

    sent = []
    for block in range(sections):
        features = lax.all_gather(current, TENSOR, axis=0, tiled=True).astype(jnp.float32)
        gain = gains[block][:, None]
        scaled = (features * gain).astype(jnp.bfloat16)
        partial = lax.dot_general(
            weights[block], scaled, (((0,), (0,)), ((), ())), preferred_element_type=jnp.float32
        )
        squares = jnp.sum(features * features, axis=0)
        piece = jnp.concatenate(
            [
                partial.reshape(dps, own, tok_group),
                jnp.broadcast_to(squares[None, None], (dps, 8, tok_group)),
            ],
            axis=1,
        )
        summed = jnp.sum(exchange(piece, "dp"), axis=0)
        rate = lax.rsqrt(summed[own : own + 1] / width_full + norm_eps)
        current = (current.astype(jnp.float32) + rate * summed[:own]).astype(jnp.bfloat16)
        normed = (features * rate * gain).astype(jnp.bfloat16)
        sent.append(
            jnp.concatenate(
                [
                    normed.reshape(dps, near * own, tok_group),
                    jnp.broadcast_to(current[None], (dps, own, tok_group)),
                ],
                axis=1,
            )
        )
    came = exchange(jnp.concatenate(sent, axis=0), PLANE)
    came = came.reshape(sections, dps, near * own + own, tok_group)
    rows = came[:, :, : near * own].reshape(sections, dps, near, own, tok_group)
    rows = rows.transpose(2, 1, 3, 0, 4).reshape(rows_local, token_total)
    result = came[:, :, near * own :].transpose(0, 3, 1, 2).reshape(token_total, width_local)
    residue = result.astype(jnp.float32) - target_all
    delta = (error_scale / token_total**0.5 * residue).astype(jnp.bfloat16)
    grad_w = jnp.dot(rows, delta, preferred_element_type=jnp.float32)
    polarity = 2.0 * soft_part - 1.0
    grad = soft_slope * (channel_scale * grad_w - 8.0 * reg_weight * polarity**3)
    sums = jnp.stack(
        [jnp.sum(residue * residue) / dps, jnp.sum(1.0 - polarity**4), jnp.sum(grad * grad)]
    )
    sums = jnp.broadcast_to(jnp.pad(sums, (0, 5))[:, None], (8, 128))
    sums = total_over(total_over(sums, TENSOR), "dp")[:, 0]
    mean_grad = sums[2] / (width_full * width_full) + grad_eps
    rounding_next = rounding[0] - step_rate * grad * lax.rsqrt(mean_grad)
    loss_value = sums[0] / (token_total * width_full) + reg_weight * sums[1] / (
        width_full * width_full
    )
    outputs = lax.dynamic_index_in_dim(
        result.reshape(sections, dps, tok_part, width_local), dp_index, 1, keepdims=False
    )
    return (rounding_next[None], outputs.reshape(1, tok_dev, width_local), loss_value.reshape(1))


def solution(mesh):
    torus = Mesh(
        mesh.devices.reshape(mesh.shape["section"], mesh.shape["dp"], 16, 2),
        ("section", "dp", "tensor_0", "tensor_1"),
    )
    return jax.shard_map(
        per_device,
        mesh=torus,
        in_specs=(
            P("dp", TENSOR),
            P("section", "dp", TENSOR),
            P("section", "dp", TENSOR),
            P("section", "dp", TENSOR),
            P("section", TENSOR),
            P("section", None),
        ),
        out_specs=(P("section", "dp", TENSOR), P("section", "dp", TENSOR), P("section")),
        check_vma=False,
    )
```

```python
import functools

import jax
import jax.numpy as jnp
from jax import lax
from jax.experimental import pallas as pl
from jax.experimental.pallas import tpu as pltpu
from jax.sharding import Mesh
from jax.sharding import PartitionSpec as P

TENSOR = ("tensor_0", "tensor_1")
PLANE = ("section", "dp")
SPREAD = ("section", "tensor_1")
NEAR = ("dp", "tensor_1")

norm_eps = 1e-06
grad_eps = 1e-06
reg_weight = 0.3
step_rate = 0.25
error_scale = 600.0

RUN = 64
LANES = 128
ROWS_K = 1024
GAIN_ROWS = 16


def exchange(x, axes):
    return lax.all_to_all(x, axes, 0, 0, tiled=True)


def total_over(x, axes):
    peers = 1
    for axis in axes if isinstance(axes, tuple) else (axes,):
        peers *= lax.axis_size(axis)
    return jnp.sum(exchange(jnp.broadcast_to(x[None], (peers, *x.shape)), axes), axis=0)


def soft_round(values):
    sig = jax.nn.sigmoid(values)
    linear = 1.2 * sig - 0.1
    soft_part = jnp.clip(linear, 0.0, 1.0)
    soft_slope = jnp.where((linear > 0.0) & (linear < 1.0), 1.2 * sig * (1.0 - sig), 0.0)
    return (soft_part, soft_slope)


def low_half(shape):
    return lax.broadcasted_iota(jnp.int32, shape, 1) < RUN


def swap_halves(x):
    return pltpu.roll(x, RUN, 1)


def weight_kernel(words_ref, rounding_ref, scale_ref, gain_ref, out_ref, floors):
    chip = pl.program_id(0)
    words = words_ref[...]
    for k in range(4):
        code = lax.shift_right_logical(words, 3 * k) & 7
        floor = code.astype(jnp.float32) - 4.0
        for pair in range(2):
            floors[pair, pl.ds(k, words.shape[0], stride=4), :] = floor[
                :, pair * LANES : (pair + 1) * LANES
            ]
    scale = scale_ref[...]
    low = low_half((RUN, LANES))

    def rows(start):
        values = pl.ds(start, RUN)
        soft_part, _ = soft_round(rounding_ref[values, :])
        floor = jnp.concatenate([floors[0, values, :], floors[1, values, :]], axis=1)
        return scale * (floor + soft_part)

    for core in range(2):
        for part in range(2):
            first = rows((core * 4 + part) * RUN)
            second = rows((core * 4 + 2 + part) * RUN)
            place = pl.ds(pl.multiple_of(chip * 256 + (part * 2 + core) * RUN, RUN), RUN)
            for pair in range(2):
                a = first[:, pair * LANES : (pair + 1) * LANES]
                b = second[:, pair * LANES : (pair + 1) * LANES]
                out_ref[2 * pair, place, :] = jnp.where(low, a, swap_halves(b)).astype(jnp.bfloat16)
                out_ref[2 * pair + 1, place, :] = jnp.where(low, swap_halves(a), b).astype(
                    jnp.bfloat16
                )

    @pl.when(chip == 0)
    def _():
        for owner in range(4):
            out_ref[owner, pl.ds(ROWS_K, 3 * GAIN_ROWS), :] = gain_ref[...].astype(jnp.bfloat16)


def make_weight(words, rounding, scale, gain_terms):
    rows = ROWS_K + 3 * GAIN_ROWS
    return pl.pallas_call(
        weight_kernel,
        grid=(4,),
        in_specs=[
            pl.BlockSpec((128, 256), lambda i: (i, 0)),
            pl.BlockSpec((512, 256), lambda i: (i, 0)),
            pl.BlockSpec((1, 256), lambda i: (0, 0)),
            pl.BlockSpec((3 * GAIN_ROWS, LANES), lambda i: (0, 0)),
        ],
        out_specs=pl.BlockSpec((4, rows, LANES), lambda i: (0, 0, 0)),
        out_shape=jax.ShapeDtypeStruct((4, rows, LANES), jnp.bfloat16),
        scratch_shapes=[pltpu.VMEM((2, 512, LANES), jnp.float32)],
        name="make_weight",
    )(words, rounding, scale, gain_terms)


def block_kernel(width, place_ref, x_ref, w_ref, cur_ref, held_ref, sent_ref, spread_ref, next_ref, rate, acc, gains):
    slab = pl.program_id(0)
    owner = place_ref[0]

    @pl.when(slab == 0)
    def _():
        total = jnp.zeros((RUN, LANES), jnp.float32)
        for y in range(4):
            for z in range(16):
                value = x_ref[y, z].astype(jnp.float32)
                total += value * value
        mean_sq = jnp.sum(total, axis=1, keepdims=True) / width
        rate[...] = jnp.broadcast_to(lax.rsqrt(mean_sq + norm_eps), (RUN, LANES))
        acc[...] = jnp.zeros_like(acc)

    terms = w_ref[0, 0, pl.ds(ROWS_K, 3 * GAIN_ROWS), :].astype(jnp.float32)
    gains[...] = (
        terms[:GAIN_ROWS] + terms[GAIN_ROWS : 2 * GAIN_ROWS] + terms[2 * GAIN_ROWS :]
    )
    scale = rate[...]

    def normed(y, chip, row):
        value = x_ref[y, slab * 4 + chip].astype(jnp.float32)
        return (value * scale * gains[pl.ds(row, 1), :]).astype(jnp.bfloat16)

    total = acc[...]
    for chip in range(4):
        parts = [normed(y, chip, chip * 4 + y) for y in range(4)]
        left = jnp.concatenate(
            [
                jnp.concatenate([parts[0], parts[1]], axis=1),
                jnp.concatenate([parts[2], parts[3]], axis=1),
            ],
            axis=0,
        )
        rows = pl.ds(chip * 256, 256)
        right = jnp.concatenate([w_ref[0, 0, rows, :], w_ref[1, 0, rows, :]], axis=1)
        total += jnp.dot(left, right, preferred_element_type=jnp.float32)
        sent_ref[0, slab, pl.ds(chip * RUN, RUN), :] = normed(owner, chip, chip * 4 + owner)
    acc[...] = total

    @pl.when(slab == 3)
    def _():
        first, second = total[:RUN], total[RUN:]
        branch = jnp.where(
            low_half((RUN, LANES)),
            first[:, :LANES] + swap_halves(second[:, :LANES]),
            swap_halves(first[:, LANES:]) + second[:, LANES:],
        )
        result = (cur_ref[...].astype(jnp.float32) + branch).astype(jnp.bfloat16)
        next_ref[...] = result
        for z in range(16):
            spread_ref[z] = result
        for d in range(4):
            sent_ref[0, d, pl.ds(4 * RUN, RUN), :] = result


def run_block(block, width, place, features, weights, current, sent):
    rows = ROWS_K + 3 * GAIN_ROWS
    sent_shape = jax.ShapeDtypeStruct((4, 4, 5 * RUN, LANES), jnp.bfloat16)
    in_specs = [
        pl.BlockSpec(memory_space=pltpu.SMEM),
        pl.BlockSpec((4, 16, RUN, LANES), lambda i: (0, 0, 0, 0)),
        pl.BlockSpec((2, 1, rows, LANES), lambda i: (block, i, 0, 0)),
        pl.BlockSpec((RUN, LANES), lambda i: (0, 0)),
    ]
    operands = [place, features, weights, current]
    body = functools.partial(block_kernel, width)
    aliases = {}
    if sent is None:

        def body(place_ref, x_ref, w_ref, cur_ref, *rest):
            block_kernel(width, place_ref, x_ref, w_ref, cur_ref, None, *rest)

    else:
        in_specs.append(pl.BlockSpec(memory_space=pl.ANY))
        operands.append(sent)
        aliases = {4: 0}
    return pl.pallas_call(
        body,
        grid=(4,),
        in_specs=in_specs,
        out_specs=[
            pl.BlockSpec((1, 4, 5 * RUN, LANES), lambda i: (block, 0, 0, 0)),
            pl.BlockSpec((16, RUN, LANES), lambda i: (0, 0, 0)),
            pl.BlockSpec((RUN, LANES), lambda i: (0, 0)),
        ],
        out_shape=[
            sent_shape,
            jax.ShapeDtypeStruct((16, RUN, LANES), jnp.bfloat16),
            jax.ShapeDtypeStruct((RUN, LANES), jnp.bfloat16),
        ],
        scratch_shapes=[
            pltpu.VMEM((RUN, LANES), jnp.float32),
            pltpu.VMEM((2 * RUN, 256), jnp.float32),
            pltpu.VMEM((GAIN_ROWS, LANES), jnp.float32),
        ],
        input_output_aliases=aliases,
        name=f"block_{block}",
    )(*operands)


def grad_kernel(coef, place_ref, mine_ref, other_ref, target_ref, rounding_ref, scale_ref, grad_ref, out_ref, sums_ref, delta, stage):
    chip = pl.program_id(0)
    owner, core = place_ref[0], place_ref[1]
    sources = (mine_ref, other_ref)

    def tile_sum(x):
        return jnp.sum(x.reshape(-1, 8, x.shape[1] // LANES, LANES), axis=(0, 2))

    @pl.when(chip == 0)
    def _():
        low = low_half((RUN, LANES))
        recon = jnp.zeros((8, LANES), jnp.float32)
        for half in range(2):
            token_core = core if half == 0 else 1 - core
            for x in range(4):
                start = pl.multiple_of(x * 32 + token_core * 16, 16)
                for pair in range(2):
                    lanes = pl.ds(pair * LANES, LANES)
                    even = sources[half][x * 4 + 2 * pair, pl.ds(4 * RUN, RUN), :].astype(jnp.float32)
                    odd = sources[half][x * 4 + 2 * pair + 1, pl.ds(4 * RUN, RUN), :].astype(jnp.float32)
                    even = jnp.where(core == 0, even, swap_halves(even))
                    odd = jnp.where(core == 0, swap_halves(odd), odd)
                    result = jnp.where(low, even, odd)
                    stage[:, lanes] = result
                    goal = jnp.concatenate(
                        [
                            target_ref[y, pl.ds(start, 16), lanes].astype(jnp.float32)
                            for y in range(4)
                        ],
                        axis=0,
                    )
                    residue = result - goal
                    square = residue * residue
                    for k in range(8):
                        recon += square[8 * k : 8 * k + 8]
                    delta[pl.ds((half * 4 + x) * RUN, RUN), lanes] = (coef * residue).astype(
                        jnp.bfloat16
                    )
                own = stage[pl.ds(pl.multiple_of(owner * 16, 16), 16), :]
                out_ref[pl.ds(start, 16), :] = own.astype(jnp.bfloat16)
        sums_ref[...] = jnp.zeros_like(sums_ref)
        sums_ref[0] = recon

    error = delta[...]
    scale = scale_ref[...]
    penalty = jnp.zeros((8, LANES), jnp.float32)
    squares = jnp.zeros((8, LANES), jnp.float32)
    rows = pl.ds(pl.multiple_of(chip * RUN, RUN), RUN)
    for y in range(4):
        left = jnp.concatenate(
            [sources[half][x * 4 + y, rows, :] for half in range(2) for x in range(4)], axis=0
        )
        product = lax.dot_general(
            left, error, (((0,), (0,)), ((), ())), preferred_element_type=jnp.float32
        )
        for cs in range(2):
            place = pl.ds((cs * 4 + y) * RUN, RUN)
            soft_part, soft_slope = soft_round(rounding_ref[place, :])
            polarity = 2.0 * soft_part - 1.0
            grad = soft_slope * (
                scale * product[cs * RUN : (cs + 1) * RUN] - 8.0 * reg_weight * polarity**3
            )
            grad_ref[place, :] = grad
            square, fine = grad * grad, 1.0 - polarity**4
            for k in range(8):
                for lane in range(2):
                    cut = (slice(8 * k, 8 * k + 8), slice(lane * LANES, (lane + 1) * LANES))
                    squares += square[cut]
                    penalty += fine[cut]
    sums_ref[1] += penalty
    sums_ref[2] += squares


def make_grad(coef, place, mine, other, target, rounding, scale):
    rows, cols = rounding.shape
    return pl.pallas_call(
        functools.partial(grad_kernel, coef),
        grid=(4,),
        in_specs=[
            pl.BlockSpec(memory_space=pltpu.SMEM),
            pl.BlockSpec(mine.shape, lambda i: (0, 0, 0)),
            pl.BlockSpec(other.shape, lambda i: (0, 0, 0)),
            pl.BlockSpec(target.shape, lambda i: (0, 0, 0)),
            pl.BlockSpec((rows // 4, cols), lambda i: (i, 0)),
            pl.BlockSpec((1, cols), lambda i: (0, 0)),
        ],
        out_specs=[
            pl.BlockSpec((rows // 4, cols), lambda i: (i, 0)),
            pl.BlockSpec((128, cols), lambda i: (0, 0)),
            pl.BlockSpec((3, 8, LANES), lambda i: (0, 0, 0)),
        ],
        out_shape=[
            jax.ShapeDtypeStruct((rows, cols), jnp.float32),
            jax.ShapeDtypeStruct((128, cols), jnp.bfloat16),
            jax.ShapeDtypeStruct((3, 8, LANES), jnp.float32),
        ],
        scratch_shapes=[
            pltpu.VMEM((8 * RUN, cols), jnp.bfloat16),
            pltpu.VMEM((RUN, cols), jnp.float32),
        ],
        name="make_grad",
    )(place, mine, other, target, rounding, scale)


def per_device(activations, targets, packed_floors, rounding, scales, norm_gains):
    sections = lax.axis_size("section")
    dps = lax.axis_size("dp")
    section_index = lax.axis_index("section")
    dp_index = lax.axis_index("dp")
    core_index = lax.axis_index("tensor_1")
    tok_dev, width_local = activations.shape
    width_full = norm_gains.shape[1]
    token_total = tok_dev * dps
    place = jnp.stack([dp_index, core_index]).astype(jnp.int32)

    gain = lax.dynamic_slice_in_dim(norm_gains[0], dp_index * (width_full // dps), width_full // dps)
    gain = gain.reshape(4, 2, 4, RUN).transpose(0, 2, 1, 3).reshape(GAIN_ROWS, LANES)
    high = lax.reduce_precision(gain, 8, 7)
    middle = lax.reduce_precision(gain - high, 8, 7)
    gain_terms = jnp.concatenate([high, middle, gain - high - middle], axis=0)
    weight = make_weight(packed_floors[0], rounding[0], scales, gain_terms)
    weight = exchange(weight, "dp")
    weights = lax.all_gather(weight, SPREAD, axis=0)

    fresh = lax.dynamic_slice_in_dim(activations, section_index * 32, 32, 0)
    fresh = fresh.reshape(2, 16, 4, RUN).transpose(2, 0, 1, 3).reshape(8, 16, RUN)
    fresh = exchange(fresh, NEAR)
    current = fresh.reshape(4, 2, 16, RUN).transpose(0, 2, 1, 3).reshape(RUN, LANES)
    target_all = lax.all_gather(targets[0], "dp", axis=0)

    spread = jnp.broadcast_to(current[None], (16, RUN, LANES))
    sent = None
    for block in range(sections):
        line = exchange(spread, "tensor_0")
        features = exchange(jnp.broadcast_to(line[None], (4, *line.shape)), "dp")
        sent, spread, current = run_block(
            block, width_full, place, features, weights, current, sent
        )
    mine = exchange(sent.reshape(16, 5 * RUN, LANES), PLANE)
    other = lax.ppermute(mine, "tensor_1", [(0, 1), (1, 0)])
    grad, outputs, sums = make_grad(
        error_scale / token_total**0.5, place, mine, other, target_all, rounding[0], scales
    )
    sums = jnp.pad(jnp.sum(sums, axis=1), ((0, 5), (0, 0)))
    sums = jnp.sum(total_over(total_over(sums, NEAR), "tensor_0"), axis=1)
    mean_grad = sums[2] / (width_full * width_full) + grad_eps
    rounding_next = rounding[0] - step_rate * grad * lax.rsqrt(mean_grad)
    loss_value = sums[0] / dps / (token_total * width_full) + reg_weight * sums[1] / (
        width_full * width_full
    )
    return (rounding_next[None], outputs[None], loss_value.reshape(1))


def solution(mesh):
    torus = Mesh(
        mesh.devices.reshape(mesh.shape["section"], mesh.shape["dp"], 16, 2),
        ("section", "dp", "tensor_0", "tensor_1"),
    )
    return jax.shard_map(
        per_device,
        mesh=torus,
        in_specs=(
            P("dp", TENSOR),
            P("section", "dp", TENSOR),
            P("section", "dp", TENSOR),
            P("section", "dp", TENSOR),
            P("section", TENSOR),
            P("section", None),
        ),
        out_specs=(P("section", "dp", TENSOR), P("section", "dp", TENSOR), P("section")),
        check_vma=False,
    )
```

```python
import functools

import jax
import jax.numpy as jnp
from jax import lax
from jax.experimental import pallas as pl
from jax.experimental.pallas import tpu as pltpu
from jax.sharding import Mesh
from jax.sharding import PartitionSpec as P

TENSOR = ("line", "side", "core")
PLANE = ("section", "dp")
SPREAD = ("section", "core")
NEAR = ("side", "dp")
REST = ("side", "dp", "core")

norm_eps = 1e-06
grad_eps = 1e-06
reg_weight = 0.3
step_rate = 0.25
error_scale = 600.0

RUN = 64
LANES = 128
ROWS_K = 1024
GAIN_ROWS = 16


def exchange(x, axes):
    return lax.all_to_all(x, axes, 0, 0, tiled=True)


def total_over(x, axes, peers):
    return jnp.sum(exchange(jnp.broadcast_to(x[None], (peers, *x.shape)), axes), axis=0)


def soft_round(values):
    sig = jax.nn.sigmoid(values)
    linear = 1.2 * sig - 0.1
    soft_part = jnp.clip(linear, 0.0, 1.0)
    soft_slope = jnp.where((linear > 0.0) & (linear < 1.0), 1.2 * sig * (1.0 - sig), 0.0)
    return (soft_part, soft_slope)


def low_half(shape):
    return lax.broadcasted_iota(jnp.int32, shape, 1) < RUN


def swap_halves(x):
    return pltpu.roll(x, RUN, 1)


def weight_kernel(words_ref, rounding_ref, scale_ref, gain_ref, out_ref, floors):
    chip = pl.program_id(0)
    words = words_ref[...]
    for k in range(4):
        code = lax.shift_right_logical(words, 3 * k) & 7
        floor = code.astype(jnp.float32) - 4.0
        for pair in range(2):
            floors[pair, pl.ds(k, words.shape[0], stride=4), :] = floor[
                :, pair * LANES : (pair + 1) * LANES
            ]
    scale = scale_ref[...]
    low = low_half((RUN, LANES))

    def rows(start):
        values = pl.ds(start, RUN)
        soft_part, _ = soft_round(rounding_ref[values, :])
        floor = jnp.concatenate([floors[0, values, :], floors[1, values, :]], axis=1)
        return scale * (floor + soft_part)

    for core in range(2):
        for part in range(2):
            first = rows((core * 4 + part) * RUN)
            second = rows((core * 4 + 2 + part) * RUN)
            place = pl.ds(pl.multiple_of(chip * 256 + (part * 2 + core) * RUN, RUN), RUN)
            for pair in range(2):
                a = first[:, pair * LANES : (pair + 1) * LANES]
                b = second[:, pair * LANES : (pair + 1) * LANES]
                out_ref[2 * pair, place, :] = jnp.where(low, a, swap_halves(b)).astype(jnp.bfloat16)
                out_ref[2 * pair + 1, place, :] = jnp.where(low, swap_halves(a), b).astype(
                    jnp.bfloat16
                )

    @pl.when(chip == 0)
    def _():
        rest = gain_ref[...]
        for term in range(3):
            part = rest.astype(jnp.bfloat16)
            rest = rest - part.astype(jnp.float32)
            for owner in range(4):
                out_ref[owner, pl.ds(ROWS_K + term * GAIN_ROWS, GAIN_ROWS), :] = part


def make_weight(words, rounding, scale, gain):
    rows = ROWS_K + 3 * GAIN_ROWS
    return pl.pallas_call(
        weight_kernel,
        grid=(4,),
        in_specs=[
            pl.BlockSpec((128, 256), lambda i: (i, 0)),
            pl.BlockSpec((512, 256), lambda i: (i, 0)),
            pl.BlockSpec((1, 256), lambda i: (0, 0)),
            pl.BlockSpec((GAIN_ROWS, LANES), lambda i: (0, 0)),
        ],
        out_specs=pl.BlockSpec((4, rows, LANES), lambda i: (0, 0, 0)),
        out_shape=jax.ShapeDtypeStruct((4, rows, LANES), jnp.bfloat16),
        scratch_shapes=[pltpu.VMEM((2, 512, LANES), jnp.float32)],
        name="make_weight",
    )(words, rounding, scale, gain)


def block_kernel(first, width, place_ref, x_ref, w_ref, cur_ref, sent_ref, spread_ref, next_ref, rate, acc, gains):
    slab = pl.program_id(0)
    owner = place_ref[0]
    low = low_half((RUN, LANES))

    def features(side, line):
        if not first:
            return [x_ref[side, y, line].astype(jnp.float32) for y in range(4)]
        values = []
        for pair in range(2):
            lanes = pl.ds(pair * LANES, LANES)
            a, b = (
                jnp.concatenate(
                    [x_ref[side, y, cs, line, :, lanes].astype(jnp.float32) for y in range(4)], axis=0
                )
                for cs in range(2)
            )
            values.append(jnp.where(low, a, swap_halves(b)))
            values.append(jnp.where(low, swap_halves(a), b))
        return values

    @pl.when(slab == 0)
    def _():
        total = jnp.zeros((RUN, LANES), jnp.float32)
        for side in range(2):
            for line in range(8):
                for value in features(side, line):
                    total += value * value
        mean_sq = jnp.sum(total, axis=1, keepdims=True) / width
        rate[...] = jnp.broadcast_to(lax.rsqrt(mean_sq + norm_eps), (RUN, LANES))
        acc[...] = jnp.zeros_like(acc)

    terms = w_ref[0, 0, pl.ds(ROWS_K, 3 * GAIN_ROWS), :].astype(jnp.float32)
    gains[...] = (
        terms[:GAIN_ROWS] + terms[GAIN_ROWS : 2 * GAIN_ROWS] + terms[2 * GAIN_ROWS :]
    )
    scale = rate[...]
    total = acc[...]
    for chip in range(4):
        parts = [
            (value * scale * gains[pl.ds(chip * 4 + y, 1), :]).astype(jnp.bfloat16)
            for y, value in enumerate(features(chip % 2, slab * 2 + chip // 2))
        ]
        left = jnp.concatenate(
            [
                jnp.concatenate([parts[0], parts[1]], axis=1),
                jnp.concatenate([parts[2], parts[3]], axis=1),
            ],
            axis=0,
        )
        rows = pl.ds(chip * 256, 256)
        right = jnp.concatenate([w_ref[0, 0, rows, :], w_ref[1, 0, rows, :]], axis=1)
        total += jnp.dot(left, right, preferred_element_type=jnp.float32)
        for y in range(4):

            @pl.when(owner == y)
            def _():
                sent_ref[0, slab, pl.ds(chip * RUN, RUN), :] = parts[y]

    acc[...] = total

    @pl.when(slab == 3)
    def _():
        upper, lower = total[:RUN], total[RUN:]
        branch = jnp.where(
            low,
            upper[:, :LANES] + swap_halves(lower[:, :LANES]),
            swap_halves(upper[:, LANES:]) + lower[:, LANES:],
        )
        result = (cur_ref[...].astype(jnp.float32) + branch).astype(jnp.bfloat16)
        next_ref[...] = result
        for line in range(8):
            spread_ref[line] = result
        for d in range(4):
            sent_ref[0, d, pl.ds(4 * RUN, RUN), :] = result


def run_block(block, width, place, features, weights, current, sent):
    rows = ROWS_K + 3 * GAIN_ROWS
    in_specs = [
        pl.BlockSpec(memory_space=pltpu.SMEM),
        pl.BlockSpec(features.shape, lambda i: (0,) * features.ndim),
        pl.BlockSpec((2, 1, rows, LANES), lambda i: (block, i, 0, 0)),
        pl.BlockSpec((RUN, LANES), lambda i: (0, 0)),
    ]
    operands = [place, features, weights, current]
    body = functools.partial(block_kernel, block == 0, width)
    aliases = {}
    if block > 0:
        in_specs.append(pl.BlockSpec(memory_space=pl.ANY))
        operands.append(sent)
        aliases = {4: 0}

    def kernel(place_ref, x_ref, w_ref, cur_ref, *rest):
        body(place_ref, x_ref, w_ref, cur_ref, *rest[len(aliases) :])

    return pl.pallas_call(
        kernel,
        grid=(4,),
        in_specs=in_specs,
        out_specs=[
            pl.BlockSpec((1, 4, 5 * RUN, LANES), lambda i: (block, 0, 0, 0)),
            pl.BlockSpec((8, RUN, LANES), lambda i: (0, 0, 0)),
            pl.BlockSpec((RUN, LANES), lambda i: (0, 0)),
        ],
        out_shape=[
            jax.ShapeDtypeStruct((4, 4, 5 * RUN, LANES), jnp.bfloat16),
            jax.ShapeDtypeStruct((8, RUN, LANES), jnp.bfloat16),
            jax.ShapeDtypeStruct((RUN, LANES), jnp.bfloat16),
        ],
        scratch_shapes=[
            pltpu.VMEM((RUN, LANES), jnp.float32),
            pltpu.VMEM((2 * RUN, 256), jnp.float32),
            pltpu.VMEM((GAIN_ROWS, LANES), jnp.float32),
        ],
        input_output_aliases=aliases,
        name=f"block_{block}",
    )(*operands)


def grad_kernel(coef, place_ref, mine_ref, other_ref, target_ref, rounding_ref, scale_ref, grad_ref, out_ref, sums_ref, delta, stage, parts):
    chip = pl.program_id(0)
    owner, core = place_ref[0], place_ref[1]
    sources = (mine_ref, other_ref)

    @pl.when(chip == 0)
    def _():
        low = low_half((RUN, LANES))
        recon = jnp.zeros((8, LANES), jnp.float32)
        for half in range(2):
            token_core = core if half == 0 else 1 - core
            for x in range(4):
                start = pl.multiple_of(x * 32 + token_core * 16, 16)
                for pair in range(2):
                    lanes = pl.ds(pair * LANES, LANES)
                    even = sources[half][x * 4 + 2 * pair, pl.ds(4 * RUN, RUN), :].astype(jnp.float32)
                    odd = sources[half][x * 4 + 2 * pair + 1, pl.ds(4 * RUN, RUN), :].astype(jnp.float32)
                    even = jnp.where(core == 0, even, swap_halves(even))
                    odd = jnp.where(core == 0, swap_halves(odd), odd)
                    result = jnp.where(low, even, odd)
                    stage[:, lanes] = result
                    goal = jnp.concatenate(
                        [
                            target_ref[y, pl.ds(start, 16), lanes].astype(jnp.float32)
                            for y in range(4)
                        ],
                        axis=0,
                    )
                    residue = result - goal
                    square = residue * residue
                    for k in range(8):
                        recon += square[8 * k : 8 * k + 8]
                    delta[pl.ds((half * 4 + x) * RUN, RUN), lanes] = (coef * residue).astype(
                        jnp.bfloat16
                    )
                own = stage[pl.ds(pl.multiple_of(owner * 16, 16), 16), :]
                out_ref[pl.ds(start, 16), :] = own.astype(jnp.bfloat16)
        parts[...] = jnp.zeros_like(parts)
        parts[0] = recon

    error = delta[...]
    scale = scale_ref[...]
    penalty = jnp.zeros((8, LANES), jnp.float32)
    squares = jnp.zeros((8, LANES), jnp.float32)
    rows = pl.ds(pl.multiple_of(chip * RUN, RUN), RUN)
    for y in range(4):
        left = jnp.concatenate(
            [sources[half][x * 4 + y, rows, :] for half in range(2) for x in range(4)], axis=0
        )
        product = lax.dot_general(
            left, error, (((0,), (0,)), ((), ())), preferred_element_type=jnp.float32
        )
        for cs in range(2):
            place = pl.ds((cs * 4 + y) * RUN, RUN)
            soft_part, soft_slope = soft_round(rounding_ref[place, :])
            polarity = 2.0 * soft_part - 1.0
            grad = soft_slope * (
                scale * product[cs * RUN : (cs + 1) * RUN] - 8.0 * reg_weight * polarity**3
            )
            grad_ref[place, :] = grad
            square, fine = grad * grad, 1.0 - polarity**4
            for k in range(8):
                for lane in range(2):
                    cut = (slice(8 * k, 8 * k + 8), slice(lane * LANES, (lane + 1) * LANES))
                    squares += square[cut]
                    penalty += fine[cut]
    parts[1] += penalty
    parts[2] += squares

    @pl.when(chip == 3)
    def _():
        lane = lax.broadcasted_iota(jnp.int32, (8, LANES), 1)
        row = jnp.zeros((8, LANES), jnp.float32)
        for k in range(3):
            row = jnp.where(lane == k, jnp.sum(parts[k]), row)
        sums_ref[...] = row


def make_grad(coef, place, mine, other, target, rounding, scale):
    rows, cols = rounding.shape
    return pl.pallas_call(
        functools.partial(grad_kernel, coef),
        grid=(4,),
        in_specs=[
            pl.BlockSpec(memory_space=pltpu.SMEM),
            pl.BlockSpec(mine.shape, lambda i: (0, 0, 0)),
            pl.BlockSpec(other.shape, lambda i: (0, 0, 0)),
            pl.BlockSpec(target.shape, lambda i: (0, 0, 0)),
            pl.BlockSpec((rows // 4, cols), lambda i: (i, 0)),
            pl.BlockSpec((1, cols), lambda i: (0, 0)),
        ],
        out_specs=[
            pl.BlockSpec((rows // 4, cols), lambda i: (i, 0)),
            pl.BlockSpec((128, cols), lambda i: (0, 0)),
            pl.BlockSpec((8, LANES), lambda i: (0, 0)),
        ],
        out_shape=[
            jax.ShapeDtypeStruct((rows, cols), jnp.float32),
            jax.ShapeDtypeStruct((128, cols), jnp.bfloat16),
            jax.ShapeDtypeStruct((8, LANES), jnp.float32),
        ],
        scratch_shapes=[
            pltpu.VMEM((8 * RUN, cols), jnp.bfloat16),
            pltpu.VMEM((RUN, cols), jnp.float32),
            pltpu.VMEM((3, 8, LANES), jnp.float32),
        ],
        name="make_grad",
    )(place, mine, other, target, rounding, scale)


def per_device(activations, targets, packed_floors, rounding, scales, norm_gains):
    sections = lax.axis_size("section")
    dps = lax.axis_size("dp")
    section_index = lax.axis_index("section")
    dp_index = lax.axis_index("dp")
    core_index = lax.axis_index("core")
    tok_dev, width_local = activations.shape
    width_full = norm_gains.shape[1]
    token_total = tok_dev * dps
    place = jnp.stack([dp_index, core_index]).astype(jnp.int32)

    gain = lax.dynamic_slice_in_dim(norm_gains[0], dp_index * (width_full // dps), width_full // dps)
    gain = gain.reshape(4, 2, 4, RUN).transpose(0, 2, 1, 3).reshape(GAIN_ROWS, LANES)
    weight = make_weight(packed_floors[0], rounding[0], scales, gain)
    weight = exchange(weight, "dp")
    weights = lax.all_gather(weight, SPREAD, axis=0)

    fresh = lax.dynamic_slice_in_dim(activations, section_index * 32, 32, 0)
    line = exchange(jnp.broadcast_to(fresh[None], (8, *fresh.shape)), "line")
    line = line.reshape(8, 2, 16, 256).transpose(1, 0, 2, 3)
    features = exchange(jnp.broadcast_to(line[None], (8, *line.shape)).reshape(16, 8, 16, 256), REST)
    features = features.reshape(2, 4, 2, 8, 16, 256)
    current = lax.dynamic_slice(
        features,
        (lax.axis_index("side"), 0, 0, lax.axis_index("line"), 0, dp_index * RUN),
        (1, 4, 2, 1, 16, RUN),
    )
    current = current.reshape(4, 2, 16, RUN).transpose(0, 2, 1, 3).reshape(RUN, LANES)
    target_all = lax.all_gather(targets[0], "dp", axis=0)
    features, target_all = lax.optimization_barrier((features, target_all))

    sent = None
    for block in range(sections):
        if block > 0:
            line = exchange(spread, "line")
            features = exchange(jnp.broadcast_to(line[None], (8, *line.shape)), NEAR)
            features = features.reshape(2, 4, 8, RUN, LANES)
        sent, spread, current = run_block(
            block, width_full, place, features, weights, current, sent
        )
    mine = exchange(sent.reshape(16, 5 * RUN, LANES), PLANE)
    other = lax.ppermute(mine, "core", [(0, 1), (1, 0)])
    grad, outputs, sums = make_grad(
        error_scale / token_total**0.5, place, mine, other, target_all, rounding[0], scales
    )
    sums = total_over(total_over(sums[:1], "line", 8), REST, 16)[0]
    mean_grad = sums[2] / (width_full * width_full) + grad_eps
    rounding_next = rounding[0] - step_rate * grad * lax.rsqrt(mean_grad)
    loss_value = sums[0] / dps / (token_total * width_full) + reg_weight * sums[1] / (
        width_full * width_full
    )
    return (rounding_next[None], outputs[None], loss_value.reshape(1))


def solution(mesh):
    torus = Mesh(
        mesh.devices.reshape(mesh.shape["section"], mesh.shape["dp"], 8, 2, 2),
        ("section", "dp", "line", "side", "core"),
    )
    return jax.shard_map(
        per_device,
        mesh=torus,
        in_specs=(
            P("dp", TENSOR),
            P("section", "dp", TENSOR),
            P("section", "dp", TENSOR),
            P("section", "dp", TENSOR),
            P("section", TENSOR),
            P("section", None),
        ),
        out_specs=(P("section", "dp", TENSOR), P("section", "dp", TENSOR), P("section")),
        check_vma=False,
    )
```

```python
import functools

import jax
import jax.numpy as jnp
from jax import lax
from jax.experimental import pallas as pl
from jax.experimental.pallas import tpu as pltpu
from jax.sharding import Mesh
from jax.sharding import PartitionSpec as P

TENSOR = ("line", "side", "core")
PLANE = ("section", "dp")
SPREAD = ("section", "core")
NEAR = ("side", "dp")
REST = ("side", "dp", "core")

norm_eps = 1e-06
grad_eps = 1e-06
reg_weight = 0.3
step_rate = 0.25
error_scale = 600.0

RUN = 64
LANES = 128
ROWS_K = 1024
GAIN_ROWS = 16


def exchange(x, axes):
    return lax.all_to_all(x, axes, 0, 0, tiled=True)


def soft_round(values):
    sig = jax.nn.sigmoid(values)
    linear = 1.2 * sig - 0.1
    soft_part = jnp.clip(linear, 0.0, 1.0)
    soft_slope = jnp.where((linear > 0.0) & (linear < 1.0), 1.2 * sig * (1.0 - sig), 0.0)
    return (soft_part, soft_slope)


def low_half(shape):
    return lax.broadcasted_iota(jnp.int32, shape, 1) < RUN


def swap_halves(x):
    return pltpu.roll(x, RUN, 1)


IN_VMEM = pl.BlockSpec(memory_space=pltpu.VMEM)
IN_SMEM = pl.BlockSpec(memory_space=pltpu.SMEM)
IN_PLACE = pl.BlockSpec(memory_space=pl.ANY)


def weight_kernel(*refs):
    words_buf, rounding_buf = refs[:4], refs[4:8]
    scale_ref, gain_ref, out_ref, floors = refs[8:]
    rest = gain_ref[...]
    for term in range(3):
        part = rest.astype(jnp.bfloat16)
        rest = rest - part.astype(jnp.float32)
        for owner in range(4):
            out_ref[owner, pl.ds(ROWS_K + term * GAIN_ROWS, GAIN_ROWS), :] = part
    scale = scale_ref[...]
    low = low_half((RUN, LANES))
    for chip in range(4):
        words = words_buf[chip][...]
        for k in range(4):
            code = lax.shift_right_logical(words, 3 * k) & 7
            floor = code.astype(jnp.float32) - 4.0
            for pair in range(2):
                floors[chip, pair, pl.ds(k, 128, stride=4), :] = floor[
                    :, pair * LANES : (pair + 1) * LANES
                ]

        def rows(start):
            values = pl.ds(start, RUN)
            soft_part, _ = soft_round(rounding_buf[chip][values, :])
            floor = jnp.concatenate([floors[chip, pair, values, :] for pair in range(2)], axis=1)
            return scale * (floor + soft_part)

        for core in range(2):
            for part in range(2):
                first = rows((core * 4 + part) * RUN)
                second = rows((core * 4 + 2 + part) * RUN)
                place = pl.ds(chip * 256 + (part * 2 + core) * RUN, RUN)
                for pair in range(2):
                    a = first[:, pair * LANES : (pair + 1) * LANES]
                    b = second[:, pair * LANES : (pair + 1) * LANES]
                    out_ref[2 * pair, place, :] = jnp.where(low, a, swap_halves(b)).astype(
                        jnp.bfloat16
                    )
                    out_ref[2 * pair + 1, place, :] = jnp.where(low, swap_halves(a), b).astype(
                        jnp.bfloat16
                    )


def pieces_of(count, shape, place):
    return [pl.BlockSpec(shape, functools.partial(place, k)) for k in range(count)]


IN_VMEM = pl.BlockSpec(memory_space=pltpu.VMEM)
IN_SMEM = pl.BlockSpec(memory_space=pltpu.SMEM)
IN_PLACE = pl.BlockSpec(memory_space=pl.ANY)


def make_weight(words, rounding, scale, gain):
    shape = (4, ROWS_K + 3 * GAIN_ROWS, LANES)
    return pl.pallas_call(
        weight_kernel,
        grid=(1,),
        in_specs=pieces_of(4, (128, 256), lambda k, i: (k, 0))
        + pieces_of(4, (512, 256), lambda k, i: (k, 0))
        + [pl.BlockSpec(scale.shape, lambda i: (0, 0)), pl.BlockSpec(gain.shape, lambda i: (0, 0))],
        out_specs=pl.BlockSpec(shape, lambda i: (0, 0, 0)),
        out_shape=jax.ShapeDtypeStruct(shape, jnp.bfloat16),
        scratch_shapes=[pltpu.VMEM((4, 2, 512, LANES), jnp.float32)],
        compiler_params=pltpu.CompilerParams(vmem_limit_bytes=24 << 20),
        name="make_weight",
    )(*[words] * 4, *[rounding] * 4, scale, gain)


def block_kernel(block, width, place_ref, x_ref, w_refs, cur_ref, earlier, sent_ref, spread_ref, next_ref, normed, moved):
    moves = [
        pltpu.make_async_copy(piece, sent_ref.at[k], moved.at[k]) for k, piece in enumerate(earlier)
    ]
    for move in moves:
        move.start()
    slot = len(earlier)
    owner = place_ref[0]
    low = low_half((RUN, LANES))

    def features(chip):
        side, line = chip % 2, chip // 2
        if block > 0:
            return [x_ref[side, y, line].astype(jnp.float32) for y in range(4)]
        values = []
        for pair in range(2):
            lanes = pl.ds(pair * LANES, LANES)
            a, b = (
                jnp.concatenate(
                    [x_ref[side, y, cs, line, :, lanes].astype(jnp.float32) for y in range(4)], axis=0
                )
                for cs in range(2)
            )
            values.append(jnp.where(low, a, swap_halves(b)))
            values.append(jnp.where(low, swap_halves(a), b))
        return values

    squares = jnp.zeros((RUN, LANES), jnp.float32)
    for chip in range(16):
        for value in features(chip):
            squares += value * value
    mean_sq = jnp.sum(squares, axis=1, keepdims=True) / width
    rate = jnp.broadcast_to(lax.rsqrt(mean_sq + norm_eps), (RUN, LANES))
    total = jnp.zeros((2 * RUN, 256), jnp.float32)
    for d in range(4):
        terms = w_refs[d][0, 0, pl.ds(ROWS_K, 3 * GAIN_ROWS), :].astype(jnp.float32)
        gain = terms[:GAIN_ROWS] + terms[GAIN_ROWS : 2 * GAIN_ROWS] + terms[2 * GAIN_ROWS :]
        upper, lower = [], []
        for chip in range(4):
            parts = [
                (value * rate * gain[chip * 4 + y : chip * 4 + y + 1]).astype(jnp.bfloat16)
                for y, value in enumerate(features(d * 4 + chip))
            ]
            for y in range(4):
                normed[y, d, pl.ds(chip * RUN, RUN), :] = parts[y]
            upper += parts[:2]
            lower += parts[2:]
        left = jnp.concatenate(
            [jnp.concatenate(upper, axis=1), jnp.concatenate(lower, axis=1)], axis=0
        )
        rows = pl.ds(0, ROWS_K)
        right = jnp.concatenate([w_refs[d][0, 0, rows, :], w_refs[d][1, 0, rows, :]], axis=1)
        total += jnp.dot(left, right, preferred_element_type=jnp.float32)
        sent_ref[slot, d, pl.ds(0, 4 * RUN), :] = normed[owner, d]
    upper, lower = total[:RUN], total[RUN:]
    branch = jnp.where(
        low,
        upper[:, :LANES] + swap_halves(lower[:, :LANES]),
        swap_halves(upper[:, LANES:]) + lower[:, LANES:],
    )
    result = (cur_ref[...].astype(jnp.float32) + branch).astype(jnp.bfloat16)
    next_ref[...] = result
    for line in range(8):
        spread_ref[line] = result
    for d in range(4):
        sent_ref[slot, d, pl.ds(4 * RUN, RUN), :] = result
    for move in moves:
        move.wait()


def run_block(block, width, place, features, weights, current, earlier):
    count = len(earlier)

    def kernel(place_ref, x_ref, w0, w1, w2, w3, cur_ref, *rest):
        block_kernel(
            block, width, place_ref, x_ref, (w0, w1, w2, w3), cur_ref, [r.at[0] for r in rest[:count]], *rest[count:]
        )

    return pl.pallas_call(
        kernel,
        grid=(1,),
        in_specs=[IN_SMEM, IN_VMEM]
        + pieces_of(4, (2, 1, ROWS_K + 3 * GAIN_ROWS, LANES), lambda k, i: (block, k, 0, 0))
        + [IN_VMEM]
        + [IN_PLACE] * count,
        out_specs=[IN_VMEM] * 3,
        out_shape=[
            jax.ShapeDtypeStruct((count + 1, 4, 5 * RUN, LANES), jnp.bfloat16),
            jax.ShapeDtypeStruct((8, RUN, LANES), jnp.bfloat16),
            jax.ShapeDtypeStruct((RUN, LANES), jnp.bfloat16),
        ],
        scratch_shapes=[
            pltpu.VMEM((4, 4, 4 * RUN, LANES), jnp.bfloat16),
            pltpu.SemaphoreType.DMA((max(count, 1),)),
        ],
        compiler_params=pltpu.CompilerParams(vmem_limit_bytes=24 << 20),
        name=f"block_{block}",
    )(place, features, *[weights] * 4, current, *earlier)


def grad_kernel(coef, place_ref, mine_ref, other_ref, target_ref, rounding_ref, scale_ref, grad_ref, out_ref, sums_ref, delta, stage):
    owner, core = place_ref[0], place_ref[1]
    sources = (mine_ref, other_ref)
    low = low_half((RUN, LANES))

    def folded(total, value):
        for k in range(0, value.shape[0], 8):
            for lane in range(0, value.shape[1], LANES):
                total += value[k : k + 8, lane : lane + LANES]
        return total

    recon, penalty, squares = (jnp.zeros((8, LANES), jnp.float32) for _ in range(3))
    for half in range(2):
        token_core = core if half == 0 else 1 - core
        for x in range(4):
            start = pl.multiple_of(x * 32 + token_core * 16, 16)
            for pair in range(2):
                lanes = pl.ds(pair * LANES, LANES)
                even = sources[half][x * 4 + 2 * pair, pl.ds(4 * RUN, RUN), :].astype(jnp.float32)
                odd = sources[half][x * 4 + 2 * pair + 1, pl.ds(4 * RUN, RUN), :].astype(jnp.float32)
                even = jnp.where(core == 0, even, swap_halves(even))
                odd = jnp.where(core == 0, swap_halves(odd), odd)
                result = jnp.where(low, even, odd)
                stage[:, lanes] = result
                goal = jnp.concatenate(
                    [target_ref[y, pl.ds(start, 16), lanes].astype(jnp.float32) for y in range(4)],
                    axis=0,
                )
                residue = result - goal
                recon = folded(recon, residue * residue)
                delta[pl.ds((half * 4 + x) * RUN, RUN), lanes] = (coef * residue).astype(
                    jnp.bfloat16
                )
            own = stage[pl.ds(pl.multiple_of(owner * 16, 16), 16), :]
            out_ref[pl.ds(start, 16), :] = own.astype(jnp.bfloat16)

    error = delta[...]
    scale = scale_ref[...]
    for chip in range(4):
        left = jnp.concatenate(
            [
                jnp.concatenate(
                    [
                        sources[half][x * 4 + y, pl.ds(chip * RUN, RUN), :]
                        for half in range(2)
                        for x in range(4)
                    ],
                    axis=0,
                )
                for y in range(4)
            ],
            axis=1,
        )
        whole = lax.dot_general(
            left, error, (((0,), (0,)), ((), ())), preferred_element_type=jnp.float32
        )
        for y in range(4):
            for cs in range(2):
                place = pl.ds(chip * 512 + (cs * 4 + y) * RUN, RUN)
                product = whole[y * LANES + cs * RUN : y * LANES + (cs + 1) * RUN]
                soft_part, soft_slope = soft_round(rounding_ref[place, :])
                polarity = 2.0 * soft_part - 1.0
                grad = soft_slope * (scale * product - 8.0 * reg_weight * polarity**3)
                grad_ref[place, :] = grad
                squares = folded(squares, grad * grad)
                penalty = folded(penalty, 1.0 - polarity**4)
    lane = lax.broadcasted_iota(jnp.int32, (1, LANES), 1)
    row = jnp.zeros((1, LANES), jnp.float32)
    for k, value in enumerate((recon, penalty, squares)):
        row = jnp.where(lane == k, jnp.sum(value), row)
    for k in range(8):
        sums_ref[k] = row


def make_grad(coef, place, mine, other, target, rounding, scale):
    rows, cols = rounding.shape
    return pl.pallas_call(
        functools.partial(grad_kernel, coef),
        in_specs=[IN_SMEM] + [IN_VMEM] * 5,
        out_specs=[IN_VMEM] * 3,
        out_shape=[
            jax.ShapeDtypeStruct((rows, cols), jnp.float32),
            jax.ShapeDtypeStruct((128, cols), jnp.bfloat16),
            jax.ShapeDtypeStruct((8, 1, LANES), jnp.float32),
        ],
        scratch_shapes=[
            pltpu.VMEM((8 * RUN, cols), jnp.bfloat16),
            pltpu.VMEM((RUN, cols), jnp.float32),
        ],
        compiler_params=pltpu.CompilerParams(vmem_limit_bytes=16 << 20),
        name="make_grad",
    )(place, mine, other, target, rounding, scale)


def finish_kernel(recon_count, penalty_count, sums_ref, grad_ref, rounding_ref, out_ref, loss_ref):
    sums = jnp.sum(sums_ref[...], axis=0)
    lane = lax.broadcasted_iota(jnp.int32, sums.shape, 1)
    recon, penalty, squares = (jnp.sum(jnp.where(lane == k, sums, 0.0)) for k in range(3))
    mean_grad = jnp.full((8, 256), squares, jnp.float32) / penalty_count + grad_eps
    rate = lax.rsqrt(mean_grad)[:1]
    out_ref[...] = rounding_ref[...] - step_rate * grad_ref[...] * rate
    loss_ref[0] = recon * (1.0 / recon_count) + reg_weight * (penalty * (1.0 / penalty_count))


def finish(recon_count, penalty_count, sums, grad, rounding):
    rows, cols = rounding.shape
    part = pl.BlockSpec((rows // 2, cols), lambda i: (i, 0))
    return pl.pallas_call(
        functools.partial(finish_kernel, recon_count, penalty_count),
        grid=(2,),
        in_specs=[pl.BlockSpec(sums.shape, lambda i: (0, 0, 0)), part, part],
        out_specs=[part, IN_SMEM],
        out_shape=[
            jax.ShapeDtypeStruct(rounding.shape, jnp.float32),
            jax.ShapeDtypeStruct((1,), jnp.float32),
        ],
        compiler_params=pltpu.CompilerParams(vmem_limit_bytes=24 << 20),
        name="finish",
    )(sums, grad, rounding)


def per_device(activations, targets, packed_floors, rounding, scales, norm_gains):
    sections = lax.axis_size("section")
    dps = lax.axis_size("dp")
    section_index = lax.axis_index("section")
    dp_index = lax.axis_index("dp")
    core_index = lax.axis_index("core")
    tok_dev, width_local = activations.shape
    width_full = norm_gains.shape[1]
    token_total = tok_dev * dps
    place = jnp.stack([dp_index, core_index]).astype(jnp.int32)

    gain = lax.dynamic_slice_in_dim(norm_gains[0], dp_index * (width_full // dps), width_full // dps)
    gain = gain.reshape(4, 2, 4, RUN).transpose(0, 2, 1, 3).reshape(GAIN_ROWS, LANES)
    weight = make_weight(packed_floors[0], rounding[0], scales, gain)
    weight = exchange(weight, "dp")
    weights = lax.all_gather(weight, SPREAD, axis=0)

    fresh = lax.dynamic_slice_in_dim(activations, section_index * 32, 32, 0)
    line = exchange(jnp.broadcast_to(fresh[None], (8, *fresh.shape)), "line")
    line = line.reshape(8, 2, 16, 256).transpose(1, 0, 2, 3)
    features = exchange(jnp.broadcast_to(line[None], (8, *line.shape)).reshape(16, 8, 16, 256), REST)
    features = features.reshape(2, 4, 2, 8, 16, 256)
    current = lax.dynamic_slice(
        features,
        (lax.axis_index("side"), 0, 0, lax.axis_index("line"), 0, dp_index * RUN),
        (1, 4, 2, 1, 16, RUN),
    )
    current = current.reshape(4, 2, 16, RUN).transpose(0, 2, 1, 3).reshape(RUN, LANES)
    target_all = lax.all_gather(targets[0], "dp", axis=0)
    features, target_all = lax.optimization_barrier((features, target_all))

    pieces = []
    for block in range(sections):
        if block > 0:
            line = exchange(spread, "line")
            features = exchange(jnp.broadcast_to(line[None], (8, *line.shape)), NEAR)
            features = features.reshape(2, 4, 8, RUN, LANES)
        earlier = pieces if block == sections - 1 else []
        sent, spread, current = run_block(
            block,
            width_full,
            place,
            features,
            weights[:2] if block == 0 else weights,
            current,
            earlier,
        )
        pieces.append(sent)
    mine = exchange(sent.reshape(16, 5 * RUN, LANES), PLANE)
    other = lax.ppermute(mine, "core", [(0, 1), (1, 0)])
    grad, outputs, sums = make_grad(
        error_scale / token_total**0.5, place, mine, other, target_all, rounding[0], scales
    )
    sums = jnp.sum(exchange(sums, "line"), axis=0, keepdims=True)
    sums = exchange(jnp.broadcast_to(sums, (16, *sums.shape[1:])), REST)
    rounding_next, loss_value = finish(
        float(dps * token_total * width_full), float(width_full * width_full), sums, grad, rounding[0]
    )
    return (rounding_next[None], outputs[None], loss_value)


def solution(mesh):
    torus = Mesh(
        mesh.devices.reshape(mesh.shape["section"], mesh.shape["dp"], 8, 2, 2),
        ("section", "dp", "line", "side", "core"),
    )
    return jax.shard_map(
        per_device,
        mesh=torus,
        in_specs=(
            P("dp", TENSOR),
            P("section", "dp", TENSOR),
            P("section", "dp", TENSOR),
            P("section", "dp", TENSOR),
            P("section", TENSOR),
            P("section", None),
        ),
        out_specs=(P("section", "dp", TENSOR), P("section", "dp", TENSOR), P("section")),
        check_vma=False,
    )
```

```python
import functools

import jax
import jax.numpy as jnp
from jax import lax
from jax.experimental import pallas as pl
from jax.experimental.pallas import tpu as pltpu
from jax.sharding import Mesh
from jax.sharding import PartitionSpec as P

TENSOR = ("line", "side", "core")
PLANE = ("section", "dp")
SPREAD = ("section", "core")
NEAR = ("side", "dp")
REST = ("side", "dp", "core")

norm_eps = 1e-06
grad_eps = 1e-06
reg_weight = 0.3
step_rate = 0.25
error_scale = 600.0

RUN = 64
LANES = 128
ROWS_K = 1024
GAIN_ROWS = 16


def exchange(x, axes):
    return lax.all_to_all(x, axes, 0, 0, tiled=True)


def soft_round(values):
    sig = jax.nn.sigmoid(values)
    linear = 1.2 * sig - 0.1
    soft_part = jnp.clip(linear, 0.0, 1.0)
    soft_slope = jnp.where((linear > 0.0) & (linear < 1.0), 1.2 * sig * (1.0 - sig), 0.0)
    return (soft_part, soft_slope)


def low_half(shape):
    return lax.broadcasted_iota(jnp.int32, shape, 1) < RUN


def swap_halves(x):
    return pltpu.roll(x, RUN, 1)


IN_VMEM = pl.BlockSpec(memory_space=pltpu.VMEM)
IN_SMEM = pl.BlockSpec(memory_space=pltpu.SMEM)
IN_PLACE = pl.BlockSpec(memory_space=pl.ANY)


def weight_kernel(*refs):
    words_buf, rounding_buf = refs[:2], refs[2:4]
    scale_ref, gain_ref, out_ref, floors, gains = refs[4:]
    step = pl.program_id(0)

    @pl.when(step == 0)
    def _():
        start = lax.axis_index("dp") * (gain_ref.shape[1] // 4)
        even = low_half((8, LANES))
        for chip in range(4):
            for pair in range(2):
                a, b = (
                    jnp.broadcast_to(
                        gain_ref[
                            :,
                            pl.ds(
                                pl.multiple_of(start + chip * 512 + cs * 256 + pair * LANES, LANES),
                                LANES,
                            ),
                        ],
                        (8, LANES),
                    )
                    for cs in range(2)
                )
                row = chip * 4 + 2 * pair
                gains[pl.ds(row, 1), :] = jnp.where(even, a, swap_halves(b))[:1]
                gains[pl.ds(row + 1, 1), :] = jnp.where(even, swap_halves(a), b)[:1]
        rest = gains[...]
        for term in range(3):
            part = rest.astype(jnp.bfloat16)
            rest = rest - part.astype(jnp.float32)
            for owner in range(4):
                out_ref[owner, pl.ds(ROWS_K + term * GAIN_ROWS, GAIN_ROWS), :] = part

    scale = scale_ref[...]
    low = low_half((RUN, LANES))
    for k2 in range(2):
        words = words_buf[k2][...]
        for k in range(4):
            code = lax.shift_right_logical(words, 3 * k) & 7
            floor = code.astype(jnp.float32) - 4.0
            for pair in range(2):
                floors[k2, pair, pl.ds(k, 128, stride=4), :] = floor[
                    :, pair * LANES : (pair + 1) * LANES
                ]

        def rows(start):
            values = pl.ds(start, RUN)
            soft_part, _ = soft_round(rounding_buf[k2][values, :])
            floor = jnp.concatenate([floors[k2, pair, values, :] for pair in range(2)], axis=1)
            return scale * (floor + soft_part)

        for core in range(2):
            for part in range(2):
                first = rows((core * 4 + part) * RUN)
                second = rows((core * 4 + 2 + part) * RUN)
                place = pl.ds(
                    pl.multiple_of((2 * step + k2) * 256 + (part * 2 + core) * RUN, RUN), RUN
                )
                for pair in range(2):
                    a = first[:, pair * LANES : (pair + 1) * LANES]
                    b = second[:, pair * LANES : (pair + 1) * LANES]
                    out_ref[2 * pair, place, :] = jnp.where(low, a, swap_halves(b)).astype(
                        jnp.bfloat16
                    )
                    out_ref[2 * pair + 1, place, :] = jnp.where(low, swap_halves(a), b).astype(
                        jnp.bfloat16
                    )


def pieces_of(count, shape, place):
    return [pl.BlockSpec(shape, functools.partial(place, k)) for k in range(count)]


IN_VMEM = pl.BlockSpec(memory_space=pltpu.VMEM)
IN_SMEM = pl.BlockSpec(memory_space=pltpu.SMEM)
IN_PLACE = pl.BlockSpec(memory_space=pl.ANY)


def make_weight(words, rounding, scale, gain):
    shape = (4, ROWS_K + 3 * GAIN_ROWS, LANES)
    return pl.pallas_call(
        weight_kernel,
        grid=(2,),
        in_specs=pieces_of(2, (128, 256), lambda k, i: (2 * i + k, 0))
        + pieces_of(2, (512, 256), lambda k, i: (2 * i + k, 0))
        + [pl.BlockSpec(scale.shape, lambda i: (0, 0)), pl.BlockSpec(gain.shape, lambda i: (0, 0))],
        out_specs=pl.BlockSpec(shape, lambda i: (0, 0, 0)),
        out_shape=jax.ShapeDtypeStruct(shape, jnp.bfloat16),
        scratch_shapes=[
            pltpu.VMEM((2, 2, 512, LANES), jnp.float32),
            pltpu.VMEM((GAIN_ROWS, LANES), jnp.float32),
        ],
        name="make_weight",
    )(*[words] * 2, *[rounding] * 2, scale, gain)


def block_kernel(block, width, place_ref, x_ref, w_refs, cur_ref, earlier, sent_ref, spread_ref, next_ref, normed, moved):
    moves = [
        pltpu.make_async_copy(piece, sent_ref.at[k], moved.at[k]) for k, piece in enumerate(earlier)
    ]
    for move in moves:
        move.start()
    slot = len(earlier)
    owner = place_ref[0]
    low = low_half((RUN, LANES))

    def features(chip):
        side, line = chip % 2, chip // 2
        if block > 0:
            return [x_ref[side, y, line].astype(jnp.float32) for y in range(4)]
        values = []
        for pair in range(2):
            lanes = pl.ds(pair * LANES, LANES)
            a, b = (
                jnp.concatenate(
                    [x_ref[side, y, cs, line, :, lanes].astype(jnp.float32) for y in range(4)], axis=0
                )
                for cs in range(2)
            )
            values.append(jnp.where(low, a, swap_halves(b)))
            values.append(jnp.where(low, swap_halves(a), b))
        return values

    squares = jnp.zeros((RUN, LANES), jnp.float32)
    for chip in range(16):
        for value in features(chip):
            squares += value * value
    mean_sq = jnp.sum(squares, axis=1, keepdims=True) / width
    rate = jnp.broadcast_to(lax.rsqrt(mean_sq + norm_eps), (RUN, LANES))
    total = jnp.zeros((2 * RUN, 256), jnp.float32)
    for d in range(4):
        terms = w_refs[d][0, 0, pl.ds(ROWS_K, 3 * GAIN_ROWS), :].astype(jnp.float32)
        gain = terms[:GAIN_ROWS] + terms[GAIN_ROWS : 2 * GAIN_ROWS] + terms[2 * GAIN_ROWS :]
        upper, lower = [], []
        for chip in range(4):
            parts = [
                (value * rate * gain[chip * 4 + y : chip * 4 + y + 1]).astype(jnp.bfloat16)
                for y, value in enumerate(features(d * 4 + chip))
            ]
            for y in range(4):
                normed[y, d, pl.ds(chip * RUN, RUN), :] = parts[y]
            upper += parts[:2]
            lower += parts[2:]
        left = jnp.concatenate(
            [jnp.concatenate(upper, axis=1), jnp.concatenate(lower, axis=1)], axis=0
        )
        rows = pl.ds(0, ROWS_K)
        right = jnp.concatenate([w_refs[d][0, 0, rows, :], w_refs[d][1, 0, rows, :]], axis=1)
        total += jnp.dot(left, right, preferred_element_type=jnp.float32)
        sent_ref[slot, d, pl.ds(0, 4 * RUN), :] = normed[owner, d]
    upper, lower = total[:RUN], total[RUN:]
    branch = jnp.where(
        low,
        upper[:, :LANES] + swap_halves(lower[:, :LANES]),
        swap_halves(upper[:, LANES:]) + lower[:, LANES:],
    )
    result = (cur_ref[...].astype(jnp.float32) + branch).astype(jnp.bfloat16)
    next_ref[...] = result
    for line in range(8):
        spread_ref[line] = result
    for d in range(4):
        sent_ref[slot, d, pl.ds(4 * RUN, RUN), :] = result
    for move in moves:
        move.wait()


def run_block(block, width, place, features, weights, current, earlier):
    count = len(earlier)

    def kernel(place_ref, x_ref, w0, w1, w2, w3, cur_ref, *rest):
        block_kernel(
            block, width, place_ref, x_ref, (w0, w1, w2, w3), cur_ref, [r.at[0] for r in rest[:count]], *rest[count:]
        )

    return pl.pallas_call(
        kernel,
        grid=(1,),
        in_specs=[IN_SMEM, IN_VMEM]
        + pieces_of(4, (2, 1, ROWS_K + 3 * GAIN_ROWS, LANES), lambda k, i: (block, k, 0, 0))
        + [IN_VMEM]
        + [IN_PLACE] * count,
        out_specs=[IN_VMEM] * 3,
        out_shape=[
            jax.ShapeDtypeStruct((count + 1, 4, 5 * RUN, LANES), jnp.bfloat16),
            jax.ShapeDtypeStruct((8, RUN, LANES), jnp.bfloat16),
            jax.ShapeDtypeStruct((RUN, LANES), jnp.bfloat16),
        ],
        scratch_shapes=[
            pltpu.VMEM((4, 4, 4 * RUN, LANES), jnp.bfloat16),
            pltpu.SemaphoreType.DMA((max(count, 1),)),
        ],
        compiler_params=pltpu.CompilerParams(vmem_limit_bytes=24 << 20),
        name=f"block_{block}",
    )(place, features, *[weights] * 4, current, *earlier)


def grad_kernel(coef, place_ref, mine_ref, other_ref, target_ref, rounding_ref, scale_ref, grad_ref, out_ref, sums_ref, delta, stage):
    owner, core = place_ref[0], place_ref[1]
    sources = (mine_ref, other_ref)
    low = low_half((RUN, LANES))

    def folded(total, value):
        for k in range(0, value.shape[0], 8):
            for lane in range(0, value.shape[1], LANES):
                total += value[k : k + 8, lane : lane + LANES]
        return total

    recon, penalty, squares = (jnp.zeros((8, LANES), jnp.float32) for _ in range(3))
    for half in range(2):
        token_core = core if half == 0 else 1 - core
        for x in range(4):
            start = pl.multiple_of(x * 32 + token_core * 16, 16)
            for pair in range(2):
                lanes = pl.ds(pair * LANES, LANES)
                even = sources[half][x * 4 + 2 * pair, pl.ds(4 * RUN, RUN), :].astype(jnp.float32)
                odd = sources[half][x * 4 + 2 * pair + 1, pl.ds(4 * RUN, RUN), :].astype(jnp.float32)
                even = jnp.where(core == 0, even, swap_halves(even))
                odd = jnp.where(core == 0, swap_halves(odd), odd)
                result = jnp.where(low, even, odd)
                stage[:, lanes] = result
                goal = jnp.concatenate(
                    [target_ref[y, pl.ds(start, 16), lanes].astype(jnp.float32) for y in range(4)],
                    axis=0,
                )
                residue = result - goal
                recon = folded(recon, residue * residue)
                delta[pl.ds((half * 4 + x) * RUN, RUN), lanes] = (coef * residue).astype(
                    jnp.bfloat16
                )
            own = stage[pl.ds(pl.multiple_of(owner * 16, 16), 16), :]
            out_ref[pl.ds(start, 16), :] = own.astype(jnp.bfloat16)

    error = delta[...]
    scale = scale_ref[...]
    for chip in range(4):
        left = jnp.concatenate(
            [
                jnp.concatenate(
                    [
                        sources[half][x * 4 + y, pl.ds(chip * RUN, RUN), :]
                        for half in range(2)
                        for x in range(4)
                    ],
                    axis=0,
                )
                for y in range(4)
            ],
            axis=1,
        )
        whole = lax.dot_general(
            left, error, (((0,), (0,)), ((), ())), preferred_element_type=jnp.float32
        )
        for y in range(4):
            for cs in range(2):
                place = pl.ds(chip * 512 + (cs * 4 + y) * RUN, RUN)
                product = whole[y * LANES + cs * RUN : y * LANES + (cs + 1) * RUN]
                soft_part, soft_slope = soft_round(rounding_ref[place, :])
                polarity = 2.0 * soft_part - 1.0
                grad = soft_slope * (scale * product - 8.0 * reg_weight * polarity**3)
                grad_ref[place, :] = grad
                squares = folded(squares, grad * grad)
                penalty = folded(penalty, 1.0 - polarity**4)
    lane = lax.broadcasted_iota(jnp.int32, (1, LANES), 1)
    row = jnp.zeros((1, LANES), jnp.float32)
    for k, value in enumerate((recon, penalty, squares)):
        row = jnp.where(lane == k, jnp.sum(value), row)
    for k in range(8):
        sums_ref[k] = row


def make_grad(coef, place, mine, other, target, rounding, scale):
    rows, cols = rounding.shape
    return pl.pallas_call(
        functools.partial(grad_kernel, coef),
        in_specs=[IN_SMEM] + [IN_VMEM] * 5,
        out_specs=[IN_VMEM] * 3,
        out_shape=[
            jax.ShapeDtypeStruct((rows, cols), jnp.float32),
            jax.ShapeDtypeStruct((128, cols), jnp.bfloat16),
            jax.ShapeDtypeStruct((8, 1, LANES), jnp.float32),
        ],
        scratch_shapes=[
            pltpu.VMEM((8 * RUN, cols), jnp.bfloat16),
            pltpu.VMEM((RUN, cols), jnp.float32),
        ],
        compiler_params=pltpu.CompilerParams(vmem_limit_bytes=16 << 20),
        name="make_grad",
    )(place, mine, other, target, rounding, scale)


def add_kernel(parts_ref, out_ref):
    total = jnp.sum(parts_ref[...], axis=0, keepdims=True)
    out_ref[...] = jnp.broadcast_to(total, out_ref.shape)


def add_copies(parts, count):
    return pl.pallas_call(
        add_kernel,
        in_specs=[IN_VMEM],
        out_specs=IN_VMEM,
        out_shape=jax.ShapeDtypeStruct((count, *parts.shape[1:]), parts.dtype),
        compiler_params=pltpu.CompilerParams(vmem_limit_bytes=2 << 20),
        name="add_copies",
    )(parts)


def finish_kernel(recon_count, penalty_count, sums_ref, grad_ref, rounding_ref, out_ref, loss_ref):
    sums = jnp.sum(sums_ref[...], axis=0)
    lane = lax.broadcasted_iota(jnp.int32, sums.shape, 1)
    recon, penalty, squares = (jnp.sum(jnp.where(lane == k, sums, 0.0)) for k in range(3))
    mean_grad = jnp.full((8, 256), squares, jnp.float32) / penalty_count + grad_eps
    rate = lax.rsqrt(mean_grad)[:1]
    out_ref[...] = rounding_ref[...] - step_rate * grad_ref[...] * rate
    loss_ref[0] = recon * (1.0 / recon_count) + reg_weight * (penalty * (1.0 / penalty_count))


def finish(recon_count, penalty_count, sums, grad, rounding):
    rows, cols = rounding.shape
    part = pl.BlockSpec((rows // 2, cols), lambda i: (i, 0))
    return pl.pallas_call(
        functools.partial(finish_kernel, recon_count, penalty_count),
        grid=(2,),
        in_specs=[pl.BlockSpec(sums.shape, lambda i: (0, 0, 0)), part, part],
        out_specs=[part, IN_SMEM],
        out_shape=[
            jax.ShapeDtypeStruct(rounding.shape, jnp.float32),
            jax.ShapeDtypeStruct((1,), jnp.float32),
        ],
        compiler_params=pltpu.CompilerParams(vmem_limit_bytes=24 << 20),
        name="finish",
    )(sums, grad, rounding)


def per_device(activations, targets, packed_floors, rounding, scales, norm_gains):
    sections = lax.axis_size("section")
    dps = lax.axis_size("dp")
    section_index = lax.axis_index("section")
    dp_index = lax.axis_index("dp")
    core_index = lax.axis_index("core")
    tok_dev, width_local = activations.shape
    width_full = norm_gains.shape[1]
    token_total = tok_dev * dps
    place = jnp.stack([dp_index, core_index]).astype(jnp.int32)

    weight = make_weight(packed_floors[0], rounding[0], scales, norm_gains)
    weight = exchange(weight, "dp")
    weights = lax.all_gather(weight, SPREAD, axis=0)

    fresh = lax.dynamic_slice_in_dim(activations, section_index * 32, 32, 0)
    line = exchange(jnp.broadcast_to(fresh[None], (8, *fresh.shape)), "line")
    line = line.reshape(8, 2, 16, 256).transpose(1, 0, 2, 3)
    features = exchange(jnp.broadcast_to(line[None], (8, *line.shape)).reshape(16, 8, 16, 256), REST)
    features = features.reshape(2, 4, 2, 8, 16, 256)
    current = lax.dynamic_slice(
        features,
        (lax.axis_index("side"), 0, 0, lax.axis_index("line"), 0, dp_index * RUN),
        (1, 4, 2, 1, 16, RUN),
    )
    current = current.reshape(4, 2, 16, RUN).transpose(0, 2, 1, 3).reshape(RUN, LANES)
    target_all = lax.all_gather(targets[0], "dp", axis=0)
    features, target_all = lax.optimization_barrier((features, target_all))

    pieces = []
    for block in range(sections):
        if block > 0:
            line = exchange(spread, "line")
            features = exchange(jnp.broadcast_to(line[None], (8, *line.shape)), NEAR)
            features = features.reshape(2, 4, 8, RUN, LANES)
        earlier = pieces if block == sections - 1 else []
        sent, spread, current = run_block(
            block,
            width_full,
            place,
            features,
            weights[:2] if block == 0 else weights,
            current,
            earlier,
        )
        pieces.append(sent)
    mine = exchange(sent.reshape(16, 5 * RUN, LANES), PLANE)
    other = lax.ppermute(mine, "core", [(0, 1), (1, 0)])
    grad, outputs, sums = make_grad(
        error_scale / token_total**0.5, place, mine, other, target_all, rounding[0], scales
    )
    sums = exchange(add_copies(exchange(sums, "line"), 16), REST)
    rounding_next, loss_value = finish(
        float(dps * token_total * width_full), float(width_full * width_full), sums, grad, rounding[0]
    )
    return (rounding_next[None], outputs[None], loss_value)


def solution(mesh):
    torus = Mesh(
        mesh.devices.reshape(mesh.shape["section"], mesh.shape["dp"], 8, 2, 2),
        ("section", "dp", "line", "side", "core"),
    )
    return jax.shard_map(
        per_device,
        mesh=torus,
        in_specs=(
            P("dp", TENSOR),
            P("section", "dp", TENSOR),
            P("section", "dp", TENSOR),
            P("section", "dp", TENSOR),
            P("section", TENSOR),
            P("section", None),
        ),
        out_specs=(P("section", "dp", TENSOR), P("section", "dp", TENSOR), P("section")),
        check_vma=False,
    )
```

```python
import functools

import jax
import jax.numpy as jnp
from jax import lax
from jax.experimental import pallas as pl
from jax.experimental.pallas import tpu as pltpu
from jax.sharding import Mesh
from jax.sharding import PartitionSpec as P

TENSOR = ("line", "side", "core")
PLANE = ("section", "dp")
SPREAD = ("section", "core")
NEAR = ("side", "dp")
REST = ("side", "dp", "core")
FAR = ("dp", "line")
CLOSE = ("side", "core")

norm_eps = 1e-06
grad_eps = 1e-06
reg_weight = 0.3
step_rate = 0.25
error_scale = 600.0

RUN = 64
LANES = 128
ROWS_K = 1024
GAIN_ROWS = 16


def exchange(x, axes):
    return lax.all_to_all(x, axes, 0, 0, tiled=True)


def soft_round(values):
    sig = jax.nn.sigmoid(values)
    linear = 1.2 * sig - 0.1
    soft_part = jnp.clip(linear, 0.0, 1.0)
    soft_slope = jnp.where((linear > 0.0) & (linear < 1.0), 1.2 * sig * (1.0 - sig), 0.0)
    return (soft_part, soft_slope)


def low_half(shape):
    return lax.broadcasted_iota(jnp.int32, shape, 1) < RUN


def swap_halves(x):
    return pltpu.roll(x, RUN, 1)


IN_VMEM = pl.BlockSpec(memory_space=pltpu.VMEM)
IN_SMEM = pl.BlockSpec(memory_space=pltpu.SMEM)
IN_PLACE = pl.BlockSpec(memory_space=pl.ANY)


def weight_kernel(*refs):
    words_buf, rounding_buf = refs[:4], refs[4:8]
    scale_ref, gain_ref, out_ref, floors, gains = refs[8:]
    start = lax.axis_index("dp") * (gain_ref.shape[1] // 4)
    even = low_half((8, LANES))
    for chip in range(4):
        for pair in range(2):
            a, b = (
                jnp.broadcast_to(
                    gain_ref[
                        :,
                        pl.ds(
                            pl.multiple_of(start + chip * 512 + cs * 256 + pair * LANES, LANES),
                            LANES,
                        ),
                    ],
                    (8, LANES),
                )
                for cs in range(2)
            )
            row = chip * 4 + 2 * pair
            gains[pl.ds(row, 1), :] = jnp.where(even, a, swap_halves(b))[:1]
            gains[pl.ds(row + 1, 1), :] = jnp.where(even, swap_halves(a), b)[:1]
    rest = gains[...]
    for term in range(3):
        part = rest.astype(jnp.bfloat16)
        rest = rest - part.astype(jnp.float32)
        for owner in range(4):
            out_ref[owner, pl.ds(ROWS_K + term * GAIN_ROWS, GAIN_ROWS), :] = part
    scale = scale_ref[...]
    low = low_half((RUN, LANES))
    for chip in range(4):
        words = words_buf[chip][...]
        for k in range(4):
            code = lax.shift_right_logical(words, 3 * k) & 7
            floor = code.astype(jnp.float32) - 4.0
            for pair in range(2):
                floors[chip, pair, pl.ds(k, 128, stride=4), :] = floor[
                    :, pair * LANES : (pair + 1) * LANES
                ]

        def rows(start):
            values = pl.ds(start, RUN)
            soft_part, _ = soft_round(rounding_buf[chip][values, :])
            floor = jnp.concatenate([floors[chip, pair, values, :] for pair in range(2)], axis=1)
            return scale * (floor + soft_part)

        for core in range(2):
            for part in range(2):
                first = rows((core * 4 + part) * RUN)
                second = rows((core * 4 + 2 + part) * RUN)
                place = pl.ds(chip * 256 + (part * 2 + core) * RUN, RUN)
                for pair in range(2):
                    a = first[:, pair * LANES : (pair + 1) * LANES]
                    b = second[:, pair * LANES : (pair + 1) * LANES]
                    out_ref[2 * pair, place, :] = jnp.where(low, a, swap_halves(b)).astype(
                        jnp.bfloat16
                    )
                    out_ref[2 * pair + 1, place, :] = jnp.where(low, swap_halves(a), b).astype(
                        jnp.bfloat16
                    )


def pieces_of(count, shape, place):
    return [pl.BlockSpec(shape, functools.partial(place, k)) for k in range(count)]


IN_VMEM = pl.BlockSpec(memory_space=pltpu.VMEM)
IN_SMEM = pl.BlockSpec(memory_space=pltpu.SMEM)
IN_PLACE = pl.BlockSpec(memory_space=pl.ANY)


def make_weight(words, rounding, scale, gain):
    shape = (4, ROWS_K + 3 * GAIN_ROWS, LANES)
    return pl.pallas_call(
        weight_kernel,
        grid=(1,),
        in_specs=pieces_of(4, (128, 256), lambda k, i: (k, 0))
        + pieces_of(4, (512, 256), lambda k, i: (k, 0))
        + [pl.BlockSpec(scale.shape, lambda i: (0, 0)), pl.BlockSpec(gain.shape, lambda i: (0, 0))],
        out_specs=pl.BlockSpec(shape, lambda i: (0, 0, 0)),
        out_shape=jax.ShapeDtypeStruct(shape, jnp.bfloat16),
        scratch_shapes=[
            pltpu.VMEM((4, 2, 512, LANES), jnp.float32),
            pltpu.VMEM((GAIN_ROWS, LANES), jnp.float32),
        ],
        name="make_weight",
    )(*[words] * 4, *[rounding] * 4, scale, gain)


def block_kernel(block, width, place_ref, x_ref, w_refs, cur_ref, earlier, sent_ref, spread_ref, next_ref, normed, moved):
    moves = [
        pltpu.make_async_copy(piece.at[d], sent_ref.at[k, d], moved.at[k, d])
        for k, piece in enumerate(earlier)
        for d in range(4)
    ]
    for move in moves:
        move.start()
    slot = len(earlier)
    owner = place_ref[0]
    low = low_half((RUN, LANES))

    def features(chip):
        side, line = chip % 2, chip // 2
        if block > 0:
            return [x_ref[side, y, line].astype(jnp.float32) for y in range(4)]
        values = []
        for pair in range(2):
            lanes = pl.ds(pair * LANES, LANES)
            a, b = (
                jnp.concatenate(
                    [x_ref[side, y, cs, line, :, lanes].astype(jnp.float32) for y in range(4)], axis=0
                )
                for cs in range(2)
            )
            values.append(jnp.where(low, a, swap_halves(b)))
            values.append(jnp.where(low, swap_halves(a), b))
        return values

    squares = jnp.zeros((RUN, LANES), jnp.float32)
    for chip in range(16):
        for value in features(chip):
            squares += value * value
    mean_sq = jnp.sum(squares, axis=1, keepdims=True) / width
    rate = jnp.broadcast_to(lax.rsqrt(mean_sq + norm_eps), (RUN, LANES))
    total = jnp.zeros((2 * RUN, 256), jnp.float32)
    for d in range(4):
        terms = w_refs[d][0, 0, pl.ds(ROWS_K, 3 * GAIN_ROWS), :].astype(jnp.float32)
        gain = terms[:GAIN_ROWS] + terms[GAIN_ROWS : 2 * GAIN_ROWS] + terms[2 * GAIN_ROWS :]
        upper, lower = [], []
        for chip in range(4):
            parts = [
                (value * rate * gain[chip * 4 + y : chip * 4 + y + 1]).astype(jnp.bfloat16)
                for y, value in enumerate(features(d * 4 + chip))
            ]
            for y in range(4):
                normed[y, d, pl.ds(chip * RUN, RUN), :] = parts[y]
            upper += parts[:2]
            lower += parts[2:]
        left = jnp.concatenate(
            [jnp.concatenate(upper, axis=1), jnp.concatenate(lower, axis=1)], axis=0
        )
        rows = pl.ds(0, ROWS_K)
        right = jnp.concatenate([w_refs[d][0, 0, rows, :], w_refs[d][1, 0, rows, :]], axis=1)
        total += jnp.dot(left, right, preferred_element_type=jnp.float32)
        sent_ref[slot, d, pl.ds(0, 4 * RUN), :] = normed[owner, d]
    upper, lower = total[:RUN], total[RUN:]
    branch = jnp.where(
        low,
        upper[:, :LANES] + swap_halves(lower[:, :LANES]),
        swap_halves(upper[:, LANES:]) + lower[:, LANES:],
    )
    result = (cur_ref[...].astype(jnp.float32) + branch).astype(jnp.bfloat16)
    next_ref[...] = result
    for line in range(8):
        spread_ref[line] = result
    for d in range(4):
        sent_ref[slot, d, pl.ds(4 * RUN, RUN), :] = result
    for move in moves:
        move.wait()


def run_block(block, width, place, features, weights, current, earlier):
    count = len(earlier)

    def kernel(place_ref, x_ref, w0, w1, w2, w3, cur_ref, *rest):
        block_kernel(
            block, width, place_ref, x_ref, (w0, w1, w2, w3), cur_ref, [r.at[0] for r in rest[:count]], *rest[count:]
        )

    return pl.pallas_call(
        kernel,
        grid=(1,),
        in_specs=[IN_SMEM, IN_VMEM]
        + pieces_of(4, (2, 1, ROWS_K + 3 * GAIN_ROWS, LANES), lambda k, i: (block, k, 0, 0))
        + [IN_VMEM]
        + [IN_PLACE] * count,
        out_specs=[IN_VMEM] * 3,
        out_shape=[
            jax.ShapeDtypeStruct((count + 1, 4, 5 * RUN, LANES), jnp.bfloat16),
            jax.ShapeDtypeStruct((8, RUN, LANES), jnp.bfloat16),
            jax.ShapeDtypeStruct((RUN, LANES), jnp.bfloat16),
        ],
        scratch_shapes=[
            pltpu.VMEM((4, 4, 4 * RUN, LANES), jnp.bfloat16),
            pltpu.SemaphoreType.DMA((max(count, 1), 4)),
        ],
        compiler_params=pltpu.CompilerParams(vmem_limit_bytes=24 << 20),
        name=f"block_{block}",
    )(place, features, *[weights] * 4, current, *earlier)


def grad_kernel(coef, place_ref, mine_ref, other_ref, target_ref, rounding_ref, scale_ref, grad_ref, out_ref, sums_ref, delta, stage):
    owner, core = place_ref[0], place_ref[1]
    sources = (mine_ref, other_ref)
    low = low_half((RUN, LANES))

    def folded(total, value):
        for k in range(0, value.shape[0], 8):
            for lane in range(0, value.shape[1], LANES):
                total += value[k : k + 8, lane : lane + LANES]
        return total

    recon, penalty, squares = (jnp.zeros((8, LANES), jnp.float32) for _ in range(3))
    for half in range(2):
        token_core = core if half == 0 else 1 - core
        for x in range(4):
            start = pl.multiple_of(x * 32 + token_core * 16, 16)
            for pair in range(2):
                lanes = pl.ds(pair * LANES, LANES)
                even = sources[half][x * 4 + 2 * pair, pl.ds(4 * RUN, RUN), :].astype(jnp.float32)
                odd = sources[half][x * 4 + 2 * pair + 1, pl.ds(4 * RUN, RUN), :].astype(jnp.float32)
                even = jnp.where(core == 0, even, swap_halves(even))
                odd = jnp.where(core == 0, swap_halves(odd), odd)
                result = jnp.where(low, even, odd)
                stage[:, lanes] = result
                goal = jnp.concatenate(
                    [target_ref[y, pl.ds(start, 16), lanes].astype(jnp.float32) for y in range(4)],
                    axis=0,
                )
                residue = result - goal
                recon = folded(recon, residue * residue)
                delta[pl.ds((half * 4 + x) * RUN, RUN), lanes] = (coef * residue).astype(
                    jnp.bfloat16
                )
            own = stage[pl.ds(pl.multiple_of(owner * 16, 16), 16), :]
            out_ref[pl.ds(start, 16), :] = own.astype(jnp.bfloat16)

    error = delta[...]
    scale = scale_ref[...]
    for chip in range(4):
        left = jnp.concatenate(
            [
                jnp.concatenate(
                    [
                        sources[half][x * 4 + y, pl.ds(chip * RUN, RUN), :]
                        for half in range(2)
                        for x in range(4)
                    ],
                    axis=0,
                )
                for y in range(4)
            ],
            axis=1,
        )
        whole = lax.dot_general(
            left, error, (((0,), (0,)), ((), ())), preferred_element_type=jnp.float32
        )
        for y in range(4):
            for cs in range(2):
                place = pl.ds(chip * 512 + (cs * 4 + y) * RUN, RUN)
                product = whole[y * LANES + cs * RUN : y * LANES + (cs + 1) * RUN]
                soft_part, soft_slope = soft_round(rounding_ref[place, :])
                polarity = 2.0 * soft_part - 1.0
                grad = soft_slope * (scale * product - 8.0 * reg_weight * polarity**3)
                grad_ref[place, :] = grad
                squares = folded(squares, grad * grad)
                penalty = folded(penalty, 1.0 - polarity**4)
    lane = lax.broadcasted_iota(jnp.int32, (1, LANES), 1)
    row = jnp.zeros((1, LANES), jnp.float32)
    for k, value in enumerate((recon, penalty, squares)):
        row = jnp.where(lane == k, jnp.sum(value), row)
    for k in range(32):
        sums_ref[k] = row


def make_grad(coef, place, mine, other, target, rounding, scale):
    rows, cols = rounding.shape
    return pl.pallas_call(
        functools.partial(grad_kernel, coef),
        in_specs=[IN_SMEM] + [IN_VMEM] * 5,
        out_specs=[IN_VMEM] * 3,
        out_shape=[
            jax.ShapeDtypeStruct((rows, cols), jnp.float32),
            jax.ShapeDtypeStruct((128, cols), jnp.bfloat16),
            jax.ShapeDtypeStruct((32, 1, LANES), jnp.float32),
        ],
        scratch_shapes=[
            pltpu.VMEM((8 * RUN, cols), jnp.bfloat16),
            pltpu.VMEM((RUN, cols), jnp.float32),
        ],
        compiler_params=pltpu.CompilerParams(vmem_limit_bytes=16 << 20),
        name="make_grad",
    )(place, mine, other, target, rounding, scale)


def add_kernel(parts_ref, out_ref):
    total = jnp.sum(parts_ref[...], axis=0, keepdims=True)
    out_ref[...] = jnp.broadcast_to(total, out_ref.shape)


def add_copies(parts, count):
    return pl.pallas_call(
        add_kernel,
        in_specs=[IN_VMEM],
        out_specs=IN_VMEM,
        out_shape=jax.ShapeDtypeStruct((count, *parts.shape[1:]), parts.dtype),
        compiler_params=pltpu.CompilerParams(vmem_limit_bytes=2 << 20),
        name="add_copies",
    )(parts)


def finish_kernel(recon_count, penalty_count, sums_ref, grad_ref, rounding_ref, out_ref, loss_ref):
    sums = jnp.sum(sums_ref[...], axis=0)
    lane = lax.broadcasted_iota(jnp.int32, sums.shape, 1)
    recon, penalty, squares = (jnp.sum(jnp.where(lane == k, sums, 0.0)) for k in range(3))
    mean_grad = jnp.full((8, 256), squares, jnp.float32) / penalty_count + grad_eps
    rate = lax.rsqrt(mean_grad)[:1]
    out_ref[...] = rounding_ref[...] - step_rate * grad_ref[...] * rate
    loss_ref[0] = recon * (1.0 / recon_count) + reg_weight * (penalty * (1.0 / penalty_count))


def finish(recon_count, penalty_count, sums, grad, rounding):
    rows, cols = rounding.shape
    part = pl.BlockSpec((rows // 2, cols), lambda i: (i, 0))
    return pl.pallas_call(
        functools.partial(finish_kernel, recon_count, penalty_count),
        grid=(2,),
        in_specs=[pl.BlockSpec(sums.shape, lambda i: (0, 0, 0)), part, part],
        out_specs=[part, IN_SMEM],
        out_shape=[
            jax.ShapeDtypeStruct(rounding.shape, jnp.float32),
            jax.ShapeDtypeStruct((1,), jnp.float32),
        ],
        compiler_params=pltpu.CompilerParams(vmem_limit_bytes=24 << 20),
        name="finish",
    )(sums, grad, rounding)


def per_device(activations, targets, packed_floors, rounding, scales, norm_gains):
    sections = lax.axis_size("section")
    dps = lax.axis_size("dp")
    section_index = lax.axis_index("section")
    dp_index = lax.axis_index("dp")
    core_index = lax.axis_index("core")
    tok_dev, width_local = activations.shape
    width_full = norm_gains.shape[1]
    token_total = tok_dev * dps
    place = jnp.stack([dp_index, core_index]).astype(jnp.int32)

    weight = make_weight(packed_floors[0], rounding[0], scales, norm_gains)
    weight = exchange(weight, "dp")
    weights = lax.all_gather(weight, SPREAD, axis=0)

    fresh = lax.dynamic_slice_in_dim(activations, section_index * 32, 32, 0)
    line = exchange(jnp.broadcast_to(fresh[None], (8, *fresh.shape)), "line")
    line = line.reshape(8, 2, 16, 256).transpose(1, 0, 2, 3)
    features = exchange(jnp.broadcast_to(line[None], (8, *line.shape)).reshape(16, 8, 16, 256), REST)
    features = features.reshape(2, 4, 2, 8, 16, 256)
    current = lax.dynamic_slice(
        features,
        (lax.axis_index("side"), 0, 0, lax.axis_index("line"), 0, dp_index * RUN),
        (1, 4, 2, 1, 16, RUN),
    )
    current = current.reshape(4, 2, 16, RUN).transpose(0, 2, 1, 3).reshape(RUN, LANES)
    target_all = lax.all_gather(targets[0], "dp", axis=0)
    features, target_all = lax.optimization_barrier((features, target_all))

    pieces = []
    for block in range(sections):
        if block > 0:
            line = exchange(spread, "line")
            features = exchange(jnp.broadcast_to(line[None], (8, *line.shape)), NEAR)
            features = features.reshape(2, 4, 8, RUN, LANES)
        earlier = pieces if block == sections - 1 else []
        sent, spread, current = run_block(
            block,
            width_full,
            place,
            features,
            weights[:2] if block == 0 else weights,
            current,
            earlier,
        )
        pieces.append(sent)
    mine = exchange(sent.reshape(16, 5 * RUN, LANES), PLANE)
    other = lax.ppermute(mine, "core", [(0, 1), (1, 0)])
    grad, outputs, sums = make_grad(
        error_scale / token_total**0.5, place, mine, other, target_all, rounding[0], scales
    )
    sums = exchange(add_copies(exchange(sums, FAR), 4), CLOSE)
    rounding_next, loss_value = finish(
        float(dps * token_total * width_full), float(width_full * width_full), sums, grad, rounding[0]
    )
    return (rounding_next[None], outputs[None], loss_value)


def solution(mesh):
    torus = Mesh(
        mesh.devices.reshape(mesh.shape["section"], mesh.shape["dp"], 8, 2, 2),
        ("section", "dp", "line", "side", "core"),
    )
    return jax.shard_map(
        per_device,
        mesh=torus,
        in_specs=(
            P("dp", TENSOR),
            P("section", "dp", TENSOR),
            P("section", "dp", TENSOR),
            P("section", "dp", TENSOR),
            P("section", TENSOR),
            P("section", None),
        ),
        out_specs=(P("section", "dp", TENSOR), P("section", "dp", TENSOR), P("section")),
        check_vma=False,
    )
```

```python
import functools

import jax
import jax.numpy as jnp
from jax import lax
from jax.experimental import pallas as pl
from jax.experimental.pallas import tpu as pltpu
from jax.sharding import Mesh
from jax.sharding import PartitionSpec as P

TENSOR = ("line", "side", "core")
PLANE = ("section", "dp")
SPREAD = ("section", "core")
NEAR = ("side", "dp")
REST = ("side", "dp", "core")

norm_eps = 1e-06
grad_eps = 1e-06
reg_weight = 0.3
step_rate = 0.25
error_scale = 600.0

RUN = 64
LANES = 128
ROWS_K = 1024
GAIN_ROWS = 16


def exchange(x, axes):
    return lax.all_to_all(x, axes, 0, 0, tiled=True)


def soft_round(values):
    sig = jax.nn.sigmoid(values)
    linear = 1.2 * sig - 0.1
    soft_part = jnp.clip(linear, 0.0, 1.0)
    soft_slope = jnp.where((linear > 0.0) & (linear < 1.0), 1.2 * sig * (1.0 - sig), 0.0)
    return (soft_part, soft_slope)


def low_half(shape):
    return lax.broadcasted_iota(jnp.int32, shape, 1) < RUN


def swap_halves(x):
    return pltpu.roll(x, RUN, 1)


IN_VMEM = pl.BlockSpec(memory_space=pltpu.VMEM)
IN_SMEM = pl.BlockSpec(memory_space=pltpu.SMEM)


def weight_kernel(*refs):
    words_buf, rounding_buf = refs[:2], refs[2:4]
    scale_ref, gain_ref, out_ref, floors, gains = refs[4:]
    step = pl.program_id(0)

    @pl.when(step == 0)
    def _():
        start = lax.axis_index("dp") * (gain_ref.shape[1] // 4)
        even = low_half((8, LANES))
        for chip in range(4):
            for pair in range(2):
                a, b = (
                    jnp.broadcast_to(
                        gain_ref[
                            :,
                            pl.ds(
                                pl.multiple_of(start + chip * 512 + cs * 256 + pair * LANES, LANES),
                                LANES,
                            ),
                        ],
                        (8, LANES),
                    )
                    for cs in range(2)
                )
                row = chip * 4 + 2 * pair
                gains[pl.ds(row, 1), :] = jnp.where(even, a, swap_halves(b))[:1]
                gains[pl.ds(row + 1, 1), :] = jnp.where(even, swap_halves(a), b)[:1]
        rest = gains[...]
        for term in range(3):
            part = rest.astype(jnp.bfloat16)
            rest = rest - part.astype(jnp.float32)
            for owner in range(4):
                out_ref[owner, pl.ds(ROWS_K + term * GAIN_ROWS, GAIN_ROWS), :] = part

    scale = scale_ref[...]
    low = low_half((RUN, LANES))
    for k2 in range(2):
        words = words_buf[k2][...]
        for k in range(4):
            code = lax.shift_right_logical(words, 3 * k) & 7
            floor = code.astype(jnp.float32) - 4.0
            for pair in range(2):
                floors[k2, pair, pl.ds(k, 128, stride=4), :] = floor[
                    :, pair * LANES : (pair + 1) * LANES
                ]

        def rows(start):
            values = pl.ds(start, RUN)
            soft_part, _ = soft_round(rounding_buf[k2][values, :])
            floor = jnp.concatenate([floors[k2, pair, values, :] for pair in range(2)], axis=1)
            return scale * (floor + soft_part)

        for core in range(2):
            for part in range(2):
                first = rows((core * 4 + part) * RUN)
                second = rows((core * 4 + 2 + part) * RUN)
                place = pl.ds(
                    pl.multiple_of((2 * step + k2) * 256 + (part * 2 + core) * RUN, RUN), RUN
                )
                for pair in range(2):
                    a = first[:, pair * LANES : (pair + 1) * LANES]
                    b = second[:, pair * LANES : (pair + 1) * LANES]
                    out_ref[2 * pair, place, :] = jnp.where(low, a, swap_halves(b)).astype(
                        jnp.bfloat16
                    )
                    out_ref[2 * pair + 1, place, :] = jnp.where(low, swap_halves(a), b).astype(
                        jnp.bfloat16
                    )


def pieces_of(count, shape, place):
    return [pl.BlockSpec(shape, functools.partial(place, k)) for k in range(count)]


IN_VMEM = pl.BlockSpec(memory_space=pltpu.VMEM)
IN_SMEM = pl.BlockSpec(memory_space=pltpu.SMEM)


def make_weight(words, rounding, scale, gain):
    shape = (4, ROWS_K + 3 * GAIN_ROWS, LANES)
    return pl.pallas_call(
        weight_kernel,
        grid=(2,),
        in_specs=pieces_of(2, (128, 256), lambda k, i: (2 * i + k, 0))
        + pieces_of(2, (512, 256), lambda k, i: (2 * i + k, 0))
        + [pl.BlockSpec(scale.shape, lambda i: (0, 0)), pl.BlockSpec(gain.shape, lambda i: (0, 0))],
        out_specs=pl.BlockSpec(shape, lambda i: (0, 0, 0)),
        out_shape=jax.ShapeDtypeStruct(shape, jnp.bfloat16),
        scratch_shapes=[
            pltpu.VMEM((2, 2, 512, LANES), jnp.float32),
            pltpu.VMEM((GAIN_ROWS, LANES), jnp.float32),
        ],
        name="make_weight",
    )(*[words] * 2, *[rounding] * 2, scale, gain)


def block_kernel(block, width, place_ref, x_ref, w_refs, cur_ref, earlier, sent_ref, spread_ref, next_ref, normed):
    for k, piece in enumerate(earlier):
        sent_ref[k] = piece[...]
    slot = len(earlier)
    owner = place_ref[0]
    low = low_half((RUN, LANES))

    def features(chip):
        side, line = chip % 2, chip // 2
        if block > 0:
            return [x_ref[side, y, line].astype(jnp.float32) for y in range(4)]
        values = []
        for pair in range(2):
            lanes = pl.ds(pair * LANES, LANES)
            a, b = (
                jnp.concatenate(
                    [x_ref[side, y, cs, line, :, lanes].astype(jnp.float32) for y in range(4)], axis=0
                )
                for cs in range(2)
            )
            values.append(jnp.where(low, a, swap_halves(b)))
            values.append(jnp.where(low, swap_halves(a), b))
        return values

    squares = jnp.zeros((RUN, LANES), jnp.float32)
    for chip in range(16):
        for value in features(chip):
            squares += value * value
    mean_sq = jnp.sum(squares, axis=1, keepdims=True) / width
    rate = jnp.broadcast_to(lax.rsqrt(mean_sq + norm_eps), (RUN, LANES))
    total = jnp.zeros((2 * RUN, 256), jnp.float32)
    for d in range(4):
        terms = w_refs[d][0, 0, pl.ds(ROWS_K, 3 * GAIN_ROWS), :].astype(jnp.float32)
        gain = terms[:GAIN_ROWS] + terms[GAIN_ROWS : 2 * GAIN_ROWS] + terms[2 * GAIN_ROWS :]
        upper, lower = [], []
        for chip in range(4):
            parts = [
                (value * rate * gain[chip * 4 + y : chip * 4 + y + 1]).astype(jnp.bfloat16)
                for y, value in enumerate(features(d * 4 + chip))
            ]
            for y in range(4):
                normed[y, d, pl.ds(chip * RUN, RUN), :] = parts[y]
            upper += parts[:2]
            lower += parts[2:]
        left = jnp.concatenate(
            [jnp.concatenate(upper, axis=1), jnp.concatenate(lower, axis=1)], axis=0
        )
        rows = pl.ds(0, ROWS_K)
        right = jnp.concatenate([w_refs[d][0, 0, rows, :], w_refs[d][1, 0, rows, :]], axis=1)
        total += jnp.dot(left, right, preferred_element_type=jnp.float32)
        sent_ref[slot, d, pl.ds(0, 4 * RUN), :] = normed[owner, d]
    upper, lower = total[:RUN], total[RUN:]
    branch = jnp.where(
        low,
        upper[:, :LANES] + swap_halves(lower[:, :LANES]),
        swap_halves(upper[:, LANES:]) + lower[:, LANES:],
    )
    result = (cur_ref[...].astype(jnp.float32) + branch).astype(jnp.bfloat16)
    next_ref[...] = result
    for line in range(8):
        spread_ref[line] = result
    for d in range(4):
        sent_ref[slot, d, pl.ds(4 * RUN, RUN), :] = result


def run_block(block, width, place, features, weights, current, earlier):
    count = len(earlier)

    def kernel(place_ref, x_ref, w0, w1, w2, w3, cur_ref, *rest):
        block_kernel(
            block, width, place_ref, x_ref, (w0, w1, w2, w3), cur_ref, [r.at[0] for r in rest[:count]], *rest[count:]
        )

    return pl.pallas_call(
        kernel,
        grid=(1,),
        in_specs=[IN_SMEM, IN_VMEM]
        + pieces_of(4, (2, 1, ROWS_K + 3 * GAIN_ROWS, LANES), lambda k, i: (block, k, 0, 0))
        + [IN_VMEM]
        + [IN_VMEM] * count,
        out_specs=[IN_VMEM] * 3,
        out_shape=[
            jax.ShapeDtypeStruct((count + 1, 4, 5 * RUN, LANES), jnp.bfloat16),
            jax.ShapeDtypeStruct((8, RUN, LANES), jnp.bfloat16),
            jax.ShapeDtypeStruct((RUN, LANES), jnp.bfloat16),
        ],
        scratch_shapes=[
            pltpu.VMEM((4, 4, 4 * RUN, LANES), jnp.bfloat16),
        ],
        compiler_params=pltpu.CompilerParams(vmem_limit_bytes=24 << 20),
        name=f"block_{block}",
    )(place, features, *[weights] * 4, current, *earlier)


def grad_kernel(coef, place_ref, mine_ref, other_ref, target_ref, rounding_ref, scale_ref, grad_ref, out_ref, sums_ref, delta, stage):
    owner, core = place_ref[0], place_ref[1]
    sources = (mine_ref, other_ref)
    low = low_half((RUN, LANES))

    def folded(total, value):
        for k in range(0, value.shape[0], 8):
            for lane in range(0, value.shape[1], LANES):
                total += value[k : k + 8, lane : lane + LANES]
        return total

    recon, penalty, squares = (jnp.zeros((8, LANES), jnp.float32) for _ in range(3))
    for half in range(2):
        token_core = core if half == 0 else 1 - core
        for x in range(4):
            start = pl.multiple_of(x * 32 + token_core * 16, 16)
            for pair in range(2):
                lanes = pl.ds(pair * LANES, LANES)
                even = sources[half][x * 4 + 2 * pair, pl.ds(4 * RUN, RUN), :].astype(jnp.float32)
                odd = sources[half][x * 4 + 2 * pair + 1, pl.ds(4 * RUN, RUN), :].astype(jnp.float32)
                even = jnp.where(core == 0, even, swap_halves(even))
                odd = jnp.where(core == 0, swap_halves(odd), odd)
                result = jnp.where(low, even, odd)
                stage[:, lanes] = result
                goal = jnp.concatenate(
                    [target_ref[y, pl.ds(start, 16), lanes].astype(jnp.float32) for y in range(4)],
                    axis=0,
                )
                residue = result - goal
                recon = folded(recon, residue * residue)
                delta[pl.ds((half * 4 + x) * RUN, RUN), lanes] = (coef * residue).astype(
                    jnp.bfloat16
                )
            own = stage[pl.ds(pl.multiple_of(owner * 16, 16), 16), :]
            out_ref[pl.ds(start, 16), :] = own.astype(jnp.bfloat16)

    error = delta[...]
    scale = scale_ref[...]
    for chip in range(4):
        left = jnp.concatenate(
            [
                jnp.concatenate(
                    [
                        sources[half][x * 4 + y, pl.ds(chip * RUN, RUN), :]
                        for half in range(2)
                        for x in range(4)
                    ],
                    axis=0,
                )
                for y in range(4)
            ],
            axis=1,
        )
        whole = lax.dot_general(
            left, error, (((0,), (0,)), ((), ())), preferred_element_type=jnp.float32
        )
        for y in range(4):
            for cs in range(2):
                place = pl.ds(chip * 512 + (cs * 4 + y) * RUN, RUN)
                product = whole[y * LANES + cs * RUN : y * LANES + (cs + 1) * RUN]
                soft_part, soft_slope = soft_round(rounding_ref[place, :])
                polarity = 2.0 * soft_part - 1.0
                grad = soft_slope * (scale * product - 8.0 * reg_weight * polarity**3)
                grad_ref[place, :] = grad
                squares = folded(squares, grad * grad)
                penalty = folded(penalty, 1.0 - polarity**4)
    lane = lax.broadcasted_iota(jnp.int32, (1, LANES), 1)
    row = jnp.zeros((1, LANES), jnp.float32)
    for k, value in enumerate((recon, penalty, squares)):
        row = jnp.where(lane == k, jnp.sum(value), row)
    for k in range(8):
        sums_ref[k] = row


def make_grad(coef, place, mine, other, target, rounding, scale):
    rows, cols = rounding.shape
    return pl.pallas_call(
        functools.partial(grad_kernel, coef),
        in_specs=[IN_SMEM] + [IN_VMEM] * 5,
        out_specs=[IN_VMEM] * 3,
        out_shape=[
            jax.ShapeDtypeStruct((rows, cols), jnp.float32),
            jax.ShapeDtypeStruct((128, cols), jnp.bfloat16),
            jax.ShapeDtypeStruct((8, 1, LANES), jnp.float32),
        ],
        scratch_shapes=[
            pltpu.VMEM((8 * RUN, cols), jnp.bfloat16),
            pltpu.VMEM((RUN, cols), jnp.float32),
        ],
        compiler_params=pltpu.CompilerParams(vmem_limit_bytes=16 << 20),
        name="make_grad",
    )(place, mine, other, target, rounding, scale)


def add_kernel(parts_ref, out_ref):
    total = jnp.sum(parts_ref[...], axis=0, keepdims=True)
    out_ref[...] = jnp.broadcast_to(total, out_ref.shape)


def add_copies(parts, count):
    return pl.pallas_call(
        add_kernel,
        in_specs=[IN_VMEM],
        out_specs=IN_VMEM,
        out_shape=jax.ShapeDtypeStruct((count, *parts.shape[1:]), parts.dtype),
        compiler_params=pltpu.CompilerParams(vmem_limit_bytes=2 << 20),
        name="add_copies",
    )(parts)


def finish_kernel(recon_count, penalty_count, sums_ref, grad_ref, rounding_ref, out_ref, loss_ref):
    sums = jnp.sum(sums_ref[...], axis=0)
    lane = lax.broadcasted_iota(jnp.int32, sums.shape, 1)
    recon, penalty, squares = (jnp.sum(jnp.where(lane == k, sums, 0.0)) for k in range(3))
    mean_grad = jnp.full((8, 256), squares, jnp.float32) / penalty_count + grad_eps
    rate = lax.rsqrt(mean_grad)[:1]
    out_ref[...] = rounding_ref[...] - step_rate * grad_ref[...] * rate
    loss_ref[0] = recon * (1.0 / recon_count) + reg_weight * (penalty * (1.0 / penalty_count))


def finish(recon_count, penalty_count, sums, grad, rounding):
    rows, cols = rounding.shape
    part = pl.BlockSpec((rows // 2, cols), lambda i: (i, 0))
    return pl.pallas_call(
        functools.partial(finish_kernel, recon_count, penalty_count),
        grid=(2,),
        in_specs=[pl.BlockSpec(sums.shape, lambda i: (0, 0, 0)), part, part],
        out_specs=[part, IN_SMEM],
        out_shape=[
            jax.ShapeDtypeStruct(rounding.shape, jnp.float32),
            jax.ShapeDtypeStruct((1,), jnp.float32),
        ],
        compiler_params=pltpu.CompilerParams(vmem_limit_bytes=24 << 20),
        name="finish",
    )(sums, grad, rounding)


def per_device(activations, targets, packed_floors, rounding, scales, norm_gains):
    sections = lax.axis_size("section")
    dps = lax.axis_size("dp")
    section_index = lax.axis_index("section")
    dp_index = lax.axis_index("dp")
    core_index = lax.axis_index("core")
    tok_dev, width_local = activations.shape
    width_full = norm_gains.shape[1]
    token_total = tok_dev * dps
    place = jnp.stack([dp_index, core_index]).astype(jnp.int32)

    weight = make_weight(packed_floors[0], rounding[0], scales, norm_gains)
    weight = exchange(weight, "dp")
    weights = lax.all_gather(weight, SPREAD, axis=0)

    fresh = lax.dynamic_slice_in_dim(activations, section_index * 32, 32, 0)
    line = exchange(jnp.broadcast_to(fresh[None], (8, *fresh.shape)), "line")
    line = line.reshape(8, 2, 16, 256).transpose(1, 0, 2, 3)
    features = exchange(jnp.broadcast_to(line[None], (8, *line.shape)).reshape(16, 8, 16, 256), REST)
    features = features.reshape(2, 4, 2, 8, 16, 256)
    current = lax.dynamic_slice(
        features,
        (lax.axis_index("side"), 0, 0, lax.axis_index("line"), 0, dp_index * RUN),
        (1, 4, 2, 1, 16, RUN),
    )
    current = current.reshape(4, 2, 16, RUN).transpose(0, 2, 1, 3).reshape(RUN, LANES)
    target_all = lax.all_gather(targets[0], "dp", axis=0)
    features, target_all = lax.optimization_barrier((features, target_all))

    pieces = []
    for block in range(sections):
        if block > 0:
            line = exchange(spread, "line")
            features = exchange(jnp.broadcast_to(line[None], (8, *line.shape)), NEAR)
            features = features.reshape(2, 4, 8, RUN, LANES)
        earlier = pieces if block == sections - 1 else []
        sent, spread, current = run_block(
            block,
            width_full,
            place,
            features,
            weights[:2] if block == 0 else weights,
            current,
            earlier,
        )
        pieces.append(sent)
    mine = exchange(sent.reshape(16, 5 * RUN, LANES), PLANE)
    other = lax.ppermute(mine, "core", [(0, 1), (1, 0)])
    grad, outputs, sums = make_grad(
        error_scale / token_total**0.5, place, mine, other, target_all, rounding[0], scales
    )
    sums = exchange(add_copies(exchange(sums, "line"), 16), REST)
    rounding_next, loss_value = finish(
        float(dps * token_total * width_full), float(width_full * width_full), sums, grad, rounding[0]
    )
    return (rounding_next[None], outputs[None], loss_value)


def solution(mesh):
    torus = Mesh(
        mesh.devices.reshape(mesh.shape["section"], mesh.shape["dp"], 8, 2, 2),
        ("section", "dp", "line", "side", "core"),
    )
    return jax.shard_map(
        per_device,
        mesh=torus,
        in_specs=(
            P("dp", TENSOR),
            P("section", "dp", TENSOR),
            P("section", "dp", TENSOR),
            P("section", "dp", TENSOR),
            P("section", TENSOR),
            P("section", None),
        ),
        out_specs=(P("section", "dp", TENSOR), P("section", "dp", TENSOR), P("section")),
        check_vma=False,
    )
```
